32 devices in a mesh: dp: 16 (over z, x, core), tensor: 2 (over y).
Axes of the slice: x: 2, y: 2, z: 4, core: 2. Of those that a mesh axis runs over, the one named last changes fastest.
Arguments:
- inputs: bfloat16 [16384, 1024], P(('dp', 'tensor')), may hold values from -6 to 6
- seg_ids: int32 [32, 512], P('dp'), may hold values from 0 to 15, never falling along the last dimension, each value on 1 to 384 neighbouring positions
- qkv_weight: float32 [2, 3, 1024, 1024], P(None, None, 'dp', 'tensor'), may hold values from -0.1875 to 0.1875
- out_weight: float32 [2, 1024, 1024], P(None, 'tensor', 'dp'), may hold values from -1.5 to 1.5
- up_weight: float32 [2, 1024, 4096], P(None, 'dp', 'tensor'), may hold values from -0.1875 to 0.1875
- down_weight: float32 [2, 4096, 1024], P(None, 'tensor', 'dp'), may hold values from -0.09375 to 0.09375
- norm_gains: float32 [2, 2, 1024], P(None, None, ('dp', 'tensor')), may hold values from 0.5 to 1.5
- row_biases: float32 [2, 6, 1024], P(None, None, ('dp', 'tensor')), may hold values from -2.5 to 2.5
- ff_bias: float32 [2, 4096], P(None, ('dp', 'tensor')), may hold values from -2.5 to 2.5
- cotangent: float32 [16384, 1024], P(('dp', 'tensor')), may hold values from -6 to 6
Outputs:
- outputs: bfloat16 [16384, 1024], P(('dp', 'tensor'))
- input_grad: float32 [16384, 1024], P(('dp', 'tensor'))
- qkv_grad: float32 [2, 3, 1024, 1024], P(None, None, 'dp', 'tensor')
- out_grad: float32 [2, 1024, 1024], P(None, 'tensor', 'dp')
- up_grad: float32 [2, 1024, 4096], P(None, 'dp', 'tensor')
- down_grad: float32 [2, 4096, 1024], P(None, 'tensor', 'dp')
- gains_grad: float32 [2, 2, 1024], P(None, None, ('dp', 'tensor'))
- biases_grad: float32 [2, 6, 1024], P(None, None, ('dp', 'tensor'))
- ff_bias_grad: float32 [2, 4096], P(None, ('dp', 'tensor'))
The draws below stay inside these ranges and needn't reach their ends.
Inputs may be any that keep to these rules, and one draw needn't show every extreme that they name: `seg_ids`: within each sequence the document numbers never fall, and each document has 1 to 384 positions.
All inputs are finite; a program needn't handle non-finite values.
Results may differ from the reference program's by a relative error of at most 0.035.
Values may be sent and summed in bfloat16 or wider, within the bound.
No kernel may reach another device: no remote copies, remote signals or barrier semaphores. Data moves between devices by JAX's collectives and lax.ppermute only.
A program may use at most 256 MiB of HBM per device.

```python
import math
import jax
import jax.numpy as jnp
import numpy as np
from jax import lax

D = 1024
HEADS = 16
HD = 64
FF = 4096
LAYERS = 2
SEQ_LEN = 512
DOCS = 16
DOC_MOST = 384
SEQS = 32
TOKENS = 16384


def block_scale(key, extent, split, low, high):
    def one(dim, shards_of):
        heights = jax.random.uniform(jax.random.fold_in(jax.random.fold_in(key, 6), dim), (shards_of,), jnp.float32, low / len(split), high / len(split))
        return jnp.repeat(jnp.exp(heights), extent[dim] // shards_of).reshape((-1,) + (1,) * (len(extent) - dim - 1))

    level = one(*split[0])
    for cut in split[1:]:
        level = level * one(*cut)
    return level


def length_profile(count, total, limit, lean):
    weights = [(1 << 20) // math.isqrt(grade ** lean) + 1 for grade in range(2, count + 1)]
    surplus, given = total - limit - (count - 1), [1] * (count - 1)
    while surplus > 0:
        movable = [i for i in range(count - 1) if given[i] < limit]
        pool, remaining = sum([weights[i] for i in movable]), surplus
        for i in movable:
            extra = min(limit - given[i], max(1, remaining * weights[i] // pool), surplus)
            given[i] = given[i] + extra
            surplus = surplus - extra
    return np.array([limit] + given)


def ragged_sizes(own_key, count, total, bound, skew):
    if count == 2:
        one = jax.random.randint(own_key, (), max(1, total - bound), min(bound, total - 1) + 1)
        return jnp.stack([one, total - one])
    sizes = jnp.asarray(length_profile(count, total, bound, skew), jnp.int32)
    twos = (count - 1) // 2
    giver, receiver = sizes[1:1 + 2 * twos:2], sizes[2:2 + 2 * twos:2]
    room = jnp.minimum(giver - 1, bound - receiver)
    shifted = jax.random.randint(jax.random.fold_in(own_key, 1), (twos,), 0, 1 << 20) % (room + 1)
    sizes = sizes.at[1:1 + 2 * twos:2].set(giver - shifted).at[2:2 + 2 * twos:2].set(receiver + shifted)
    return sizes[jax.random.permutation(jax.random.fold_in(own_key, 2), count)]


def bell_draw(own_key, extent, width, bound, cuts=(), dtype=jnp.bfloat16):
    loudness = block_scale(own_key, extent, cuts, -0.22, 0.18) if cuts else 1.0
    entries = jax.random.normal(own_key, extent, jnp.float32) * width * loudness
    return jnp.minimum(jnp.maximum(entries, -bound), bound).astype(dtype)


def setup_inputs(seed: int = 0) -> dict:
    splits = jax.random.split(jax.random.key(seed), 11)
    inputs = bell_draw(splits[0], (TOKENS, D), 1.0, 6.0, ((0, 32),))
    seg_ids = jax.vmap(lambda own: jnp.searchsorted(jnp.cumsum(ragged_sizes(own, DOCS, SEQ_LEN, DOC_MOST, 2)), jnp.arange(SEQ_LEN), side="right"))(jax.random.split(splits[1], SEQS)).reshape((SEQS, SEQ_LEN)).astype(jnp.int32)
    qkv_weight = bell_draw(splits[2], (LAYERS, 3, D, D), D ** -0.5, 0.1875, ((2, 16), (3, 2)), jnp.float32)
    out_weight = bell_draw(splits[3], (LAYERS, D, D), (D // 64) ** -0.5, 1.5, ((1, 2), (2, 16)), jnp.float32)
    up_weight = bell_draw(splits[4], (LAYERS, D, FF), D ** -0.5, 0.1875, ((1, 16), (2, 2)), jnp.float32)
    down_weight = bell_draw(splits[5], (LAYERS, FF, D), FF ** -0.5, 0.09375, ((1, 2), (2, 16)), jnp.float32)
    norm_gains = jnp.clip(1.0 + 0.1 * jax.random.normal(splits[6], (LAYERS, 2, D), jnp.float32), 0.5, 1.5)
    row_biases = bell_draw(splits[7], (LAYERS, 6, D), 0.3, 2.5, ((2, 32),), jnp.float32)
    ff_bias = bell_draw(splits[8], (LAYERS, FF), 0.3, 2.5, ((1, 32),), jnp.float32)
    cotangent = bell_draw(splits[9], (TOKENS, D), 1.0, 6.0, ((0, 32),), jnp.float32)
    return dict(inputs=inputs, seg_ids=seg_ids, qkv_weight=qkv_weight, out_weight=out_weight, up_weight=up_weight, down_weight=down_weight, norm_gains=norm_gains, row_biases=row_biases, ff_bias=ff_bias, cotangent=cotangent)


EPSILON = 1e-06
PRECISION = lax.Precision.HIGHEST

@jax.custom_vjp
def low(v):
    return lax.optimization_barrier(v.astype(jnp.bfloat16)).astype(jnp.float32)

@jax.custom_vjp
def low_back(v):
    return v

def low_keep(v):
    return (low(v), None)

def low_pass(kept, grad):
    return (grad,)

def back_keep(v):
    return (v, None)

def back_low(kept, grad):
    return (low(grad),)
low.defvjp(low_keep, low_pass)
low_back.defvjp(back_keep, back_low)

def normed(summed, gain_row, shift_row):
    centre = summed - lax.optimization_barrier(jnp.mean(summed, axis=-1, keepdims=True))
    spread = lax.optimization_barrier(jnp.mean(centre * centre, axis=-1, keepdims=True))
    return centre * lax.rsqrt(spread + EPSILON) * gain_row + shift_row

def attend(queries, key_rows, values, segment):
    scores = jnp.einsum('qhe,khe->hqk', queries, key_rows, precision=PRECISION) * HD ** (-0.5)
    same_doc = segment[:, None] == segment[None, :]
    scores = low_back(jnp.where(same_doc[None], scores, -jnp.inf))
    row_max = lax.optimization_barrier(jnp.max(scores, axis=-1, keepdims=True))
    exp_scores = jnp.exp(scores - row_max)
    attn_probs = exp_scores / lax.optimization_barrier(jnp.sum(exp_scores, axis=-1, keepdims=True))
    return jnp.einsum('hqk,khe->qhe', low(attn_probs), values, precision=PRECISION)

def attend_pieces(pieces):
    return jax.checkpoint(attend)(pieces[0], pieces[1], pieces[2], pieces[3])

def encoder_layer(stream, segment, qkv_mat, out_mat, up_mat, down_mat, gain_rows, shifts, up_shift):
    row_count = stream.shape[0]
    seq_count = segment.shape[0]
    projected = jnp.einsum('rd,kdc->rkc', low(stream), low(qkv_mat), precision=PRECISION)
    queries = low(low_back(projected[:, 0] + shifts[0]))
    key_rows = low(low_back(projected[:, 1]))
    values = low(low_back(projected[:, 2] + shifts[1]))
    head_shape = (seq_count, row_count // seq_count, HEADS, HD)
    mixture = lax.map(attend_pieces, (queries.reshape(head_shape), key_rows.reshape(head_shape), values.reshape(head_shape), segment))
    mixture = low(low_back(mixture.reshape(row_count, D)))
    attended = low_back(jnp.dot(mixture, low(out_mat), precision=PRECISION)) + shifts[2]
    normed_mid = normed(stream + attended, gain_rows[0], shifts[3])
    hidden_in = low_back(jnp.dot(low(normed_mid), low(up_mat), precision=PRECISION) + up_shift)
    hidden_out = low(jax.nn.gelu(hidden_in, approximate=False))
    branch_out = low_back(jnp.dot(hidden_out, low(down_mat), precision=PRECISION)) + shifts[4]
    return normed(normed_mid + branch_out, gain_rows[1], shifts[5])

def forward(stream, segment, params):
    qkv_mat, out_mat, up_mat, down_mat, gain_rows, shift_rows, up_shifts = params
    for layer_index in range(LAYERS):
        stream = encoder_layer(stream, segment, qkv_mat[layer_index], out_mat[layer_index], up_mat[layer_index], down_mat[layer_index], gain_rows[layer_index], shift_rows[layer_index], up_shifts[layer_index])
    return stream

def reference(inputs, seg_ids, qkv_weight, out_weight, up_weight, down_weight, norm_gains, row_biases, ff_bias, cotangent):
    per_group = math.gcd(SEQS, max(1, 4096 // SEQ_LEN))
    groups = SEQS // per_group
    group_rows = per_group * SEQ_LEN
    streams = inputs.astype(jnp.float32).reshape(groups, group_rows, D)
    segments = seg_ids.reshape(groups, per_group, SEQ_LEN)
    cot_groups = cotangent.astype(jnp.float32).reshape(groups, group_rows, D)
    params = (qkv_weight.astype(jnp.float32), out_weight.astype(jnp.float32), up_weight.astype(jnp.float32), down_weight.astype(jnp.float32), norm_gains.astype(jnp.float32), row_biases.astype(jnp.float32), ff_bias.astype(jnp.float32))

    def accumulate(running, item):
        stream, segment, grad_out = item

        def whole_pass(stream_in, weights):
            return forward(stream_in, segment, weights)
        result, pullback = jax.vjp(whole_pass, stream, params)
        grad_in, grad_weights = pullback(grad_out)
        running = jax.tree.map(jnp.add, running, grad_weights)
        return (running, (result.astype(jnp.bfloat16), grad_in))
    zero_grads = jax.tree.map(jnp.zeros_like, params)
    running, (outputs_all, grad_all) = lax.scan(accumulate, zero_grads, (streams, segments, cot_groups))
    return (outputs_all.reshape(TOKENS, D), grad_all.reshape(TOKENS, D), running[0], running[1], running[2], running[3], running[4], running[5], running[6])
```

```python
from functools import partial

import jax
import jax.numpy as jnp
import numpy as np
from jax import lax
from jax.experimental import pallas as pl
from jax.experimental.pallas import tpu as pltpu
from jax.sharding import Mesh
from jax.sharding import PartitionSpec as P

HD = 64
EPSILON = 1e-06
HALF_ROOT = 0.7071067811865476
INV_ROOT_TAU = 0.3989422804014327
BF = jnp.bfloat16
F32 = jnp.float32
RANKS = ("dp", "thi", "tlo")
SPREAD = ("thi", "tlo", "dp")


def norm_parts(summed):
    centre = summed - jnp.mean(summed, axis=-1, keepdims=True)
    spread = jnp.mean(centre * centre, axis=-1, keepdims=True)
    rate = lax.rsqrt(spread + EPSILON)
    return centre * rate, rate


def norm_back(grad, unit, rate, gain):
    scaled = grad * gain
    return rate * (
        scaled
        - jnp.mean(scaled, axis=-1, keepdims=True)
        - unit * jnp.mean(scaled * unit, axis=-1, keepdims=True)
    )


def gelu_slope(hidden_in):
    return (
        0.5 * (1.0 + lax.erf(hidden_in * HALF_ROOT))
        + hidden_in * jnp.exp(-0.5 * hidden_in * hidden_in) * INV_ROOT_TAU
    )


def dot(a, b):
    return jnp.dot(a, b, preferred_element_type=F32)


def dot_nt(a, b):
    return lax.dot_general(a, b, (((1,), (1,)), ((), ())), preferred_element_type=F32)


def dot_tn(a, b):
    return lax.dot_general(a, b, (((0,), (0,)), ((), ())), preferred_element_type=F32)


def attend_kernel(q_ref, k_ref, v_ref, segq_ref, segk_ref, out_ref):
    same = segq_ref[0] == segk_ref[0]
    outs = []
    for half in range(q_ref.shape[1] // HD):
        cols = slice(half * HD, half * HD + HD)
        q = (q_ref[:, cols].astype(F32) * HD ** (-0.5)).astype(BF)
        scores = jnp.where(same, dot_nt(q, k_ref[:, cols]), -jnp.inf)
        top = jnp.max(scores, axis=-1, keepdims=True)
        weights = jnp.exp(scores - top)
        total = jnp.sum(weights, axis=-1, keepdims=True)
        probs = (weights * (1.0 / total)).astype(BF)
        outs.append(dot(probs, v_ref[:, cols]))
    out_ref[...] = jnp.concatenate(outs, axis=1).astype(BF)


def attend_back_kernel(q_ref, k_ref, v_ref, grad_ref, segq_ref, segk_ref, dq_ref, dk_ref, dv_ref):
    same = segk_ref[0] == segq_ref[0]
    dqs, dks, dvs = [], [], []
    for half in range(q_ref.shape[1] // HD):
        cols = slice(half * HD, half * HD + HD)
        q = (q_ref[:, cols].astype(F32) * HD ** (-0.5)).astype(BF)
        k, v, grad = k_ref[:, cols], v_ref[:, cols], grad_ref[:, cols]
        scores = jnp.where(same, dot_nt(k, q), -jnp.inf)
        top = jnp.max(scores, axis=0, keepdims=True)
        weights = jnp.exp(scores - top)
        probs = weights * (1.0 / jnp.sum(weights, axis=0, keepdims=True))
        dvs.append(dot(probs.astype(BF), grad))
        grad_probs = dot_nt(v, grad)
        inner = jnp.sum(grad_probs * probs, axis=0, keepdims=True)
        grad_scores = (probs * (grad_probs - inner)).astype(BF)
        dks.append(dot(grad_scores, q))
        dqs.append(dot_tn(grad_scores, k) * HD ** (-0.5))
    dq_ref[...] = jnp.concatenate(dqs, axis=1).astype(dq_ref.dtype)
    dk_ref[...] = jnp.concatenate(dks, axis=1).astype(dk_ref.dtype)
    dv_ref[...] = jnp.concatenate(dvs, axis=1).astype(dv_ref.dtype)


def pair_width(cols):
    return 128 if cols % 128 == 0 else cols


def attend(q, k, v, offsets, cols, seg_q, seg_k):
    sets = seg_q.shape[0]
    rows, keys = q.shape[0] // sets, k.shape[0] // sets
    wide = pair_width(cols)
    spec = lambda n, off: pl.BlockSpec((n, wide), lambda s, j, off=off: (s, off // wide + j))
    heads = cols // HD
    return pl.pallas_call(
        attend_kernel,
        grid=(sets, cols // wide),
        in_specs=[
            spec(rows, offsets[0]),
            spec(keys, offsets[1]),
            spec(keys, offsets[2]),
            pl.BlockSpec((1, rows, 1), lambda s, j: (s, 0, 0)),
            pl.BlockSpec((1, 1, keys), lambda s, j: (s, 0, 0)),
        ],
        out_specs=spec(rows, 0),
        out_shape=jax.ShapeDtypeStruct((q.shape[0], cols), BF),
        cost_estimate=pl.CostEstimate(
            flops=4 * heads * sets * rows * keys * HD * 4,
            bytes_accessed=8 * q.shape[0] * cols,
            transcendentals=heads * sets * rows * keys,
        ),
        name="attend",
    )(q, k, v, seg_q[:, :, None], seg_k[:, None, :])


def attend_back(q, k, v, offsets, cols, grad, seg_q, seg_k, kv_type):
    sets = seg_q.shape[0]
    rows, keys = q.shape[0] // sets, k.shape[0] // sets
    wide = pair_width(cols)
    spec = lambda n, off: pl.BlockSpec((n, wide), lambda s, j, off=off: (s, off // wide + j))
    heads = cols // HD
    return pl.pallas_call(
        attend_back_kernel,
        grid=(sets, cols // wide),
        in_specs=[
            spec(rows, offsets[0]),
            spec(keys, offsets[1]),
            spec(keys, offsets[2]),
            spec(rows, 0),
            pl.BlockSpec((1, 1, rows), lambda s, j: (s, 0, 0)),
            pl.BlockSpec((1, keys, 1), lambda s, j: (s, 0, 0)),
        ],
        out_specs=[spec(rows, 0), spec(keys, 0), spec(keys, 0)],
        out_shape=[
            jax.ShapeDtypeStruct((q.shape[0], cols), BF),
            jax.ShapeDtypeStruct((k.shape[0], cols), kv_type),
            jax.ShapeDtypeStruct((k.shape[0], cols), kv_type),
        ],
        cost_estimate=pl.CostEstimate(
            flops=10 * heads * sets * rows * keys * HD * 4,
            bytes_accessed=14 * q.shape[0] * cols,
            transcendentals=heads * sets * rows * keys,
        ),
        name="attend_back",
    )(q, k, v, grad, seg_q[:, None, :], seg_k[:, :, None])


def swap(value, mask):
    count = lax.axis_size("dp") * lax.axis_size("thi") * lax.axis_size("tlo")
    return lax.ppermute(value, RANKS, [(i, i ^ mask) for i in range(count)])


def gather_small(row):
    count = lax.axis_size("dp") * lax.axis_size("thi") * lax.axis_size("tlo")
    held, mask = row[None], 1
    while mask < count:
        held = jnp.concatenate([held, swap(held, mask)], axis=0)
        mask *= 2
    return jnp.take(held, jnp.arange(count) ^ lax.axis_index(RANKS), axis=0)


def scatter_small(parts):
    count = parts.shape[0]
    held, mask = jnp.take(parts, jnp.arange(count) ^ lax.axis_index(RANKS), axis=0), count // 2
    while mask:
        held = held[:mask] + swap(held[mask:], mask)
        mask //= 2
    return held[0]


def gather_weights(shard):
    whole = lax.all_gather(shard, SPREAD, axis=0, tiled=True)
    parts = lax.axis_size("thi") * lax.axis_size("tlo")
    return whole.reshape(parts, whole.shape[0] // parts, whole.shape[1])


def scatter_grads(parts):
    return lax.psum_scatter(
        jnp.concatenate(parts, axis=0), SPREAD, scatter_dimension=0, tiled=True
    ).astype(F32)


def on_device(
    inputs,
    seg_ids,
    qkv_weight,
    out_weight,
    up_weight,
    down_weight,
    norm_gains,
    row_biases,
    ff_bias,
    cotangent,
):
    blocks = lax.axis_size("thi") * lax.axis_size("tlo")
    sharers = lax.axis_size("tlo")
    rows, width = inputs.shape
    layers = qkv_weight.shape[0]
    head_cols = qkv_weight.shape[3]
    hidden = up_weight.shape[2]
    length = seg_ids.shape[1]
    sets = max(1, rows // length)
    T = range(blocks)

    seg_k = lax.dynamic_slice_in_dim(seg_ids, lax.axis_index("thi") * sets, sets)
    seg_q = seg_k
    if sharers > 1:
        seg_q = lax.dynamic_slice_in_dim(seg_k, lax.axis_index("tlo") * rows, rows, axis=1)

    shards = [
        (
            jnp.concatenate([qkv_weight[l, k] for k in range(3)], axis=1).astype(BF),
            jnp.concatenate(
                [out_weight[l].T, up_weight[l], down_weight[l].T], axis=1
            ).astype(BF),
        )
        for l in range(layers)
    ]
    gathered = [[None, None] for _ in range(layers)]
    small = gather_small(
        jnp.concatenate([norm_gains.reshape(-1), row_biases.reshape(-1), ff_bias.reshape(-1)])
    )
    devices = small.shape[0]
    cuts = np.cumsum([norm_gains.size, row_biases.size])
    spread_out = lambda piece, like: jnp.moveaxis(
        piece.reshape((devices,) + like.shape), 0, -2
    ).reshape(like.shape[:-1] + (devices * like.shape[-1],))
    gain_rows = spread_out(small[:, : cuts[0]], norm_gains)
    shift_rows = spread_out(small[:, cuts[0] : cuts[1]], row_biases)
    up_shifts = spread_out(small[:, cuts[1] :], ff_bias)

    weights = []
    for l in range(layers):
        if l == 0:
            qkv = gather_weights(shards[l][0])
            rest = gather_weights(shards[l][1])
        else:
            both = gather_weights(jnp.concatenate(shards[l], axis=1))
            qkv, rest = both[:, :, : 3 * head_cols], both[:, :, 3 * head_cols :]
        out = rest[:, :, :head_cols]
        up = rest[:, :, head_cols : head_cols + hidden]
        down = rest[:, :, head_cols + hidden :]
        weights.append((qkv, out, up, down))

    stream = inputs.astype(F32)
    stored = []
    for l in range(layers):
        qkv, out, up, down = weights[l]
        shifts, gains = shift_rows[l], gain_rows[l]
        low = stream.astype(BF)
        projected, kept_keys, mixture = [], [], []
        for t in T:
            shift = jnp.concatenate(
                [
                    shifts[0, t * head_cols : (t + 1) * head_cols],
                    jnp.zeros((head_cols,), F32),
                    shifts[1, t * head_cols : (t + 1) * head_cols],
                ]
            )
            mine = (dot(low, qkv[t]) + shift).astype(BF)
            projected.append(mine)
            if sharers > 1:
                kv = lax.all_gather(mine[:, head_cols:], "tlo", axis=0, tiled=True)
                offsets = (0, 0, head_cols)
            else:
                kv, offsets = mine, (0, head_cols, 2 * head_cols)
            kept_keys.append(kv)
            mixture.append(attend(mine, kv, kv, offsets, head_cols, seg_q, seg_k))
        attended = sum(dot_nt(mixture[t], out[t]) for t in T)
        unit_early, rate_early = norm_parts(stream + (attended + shifts[2]))
        mid = unit_early * gains[0] + shifts[3]
        mid_low = mid.astype(BF)
        hidden_in = [
            dot(mid_low, up[t]) + up_shifts[l, t * hidden : (t + 1) * hidden] for t in T
        ]
        hidden_out = [jax.nn.gelu(h, approximate=False).astype(BF) for h in hidden_in]
        branch = sum(dot_nt(hidden_out[t], down[t]) for t in T)
        unit_late, rate_late = norm_parts(mid + (branch + shifts[4]))
        stored.append(
            (
                low,
                projected,
                kept_keys,
                offsets,
                mixture,
                unit_early,
                rate_early,
                mid_low,
                hidden_in,
                hidden_out,
                unit_late,
                rate_late,
            )
        )
        stream = unit_late * gains[1] + shifts[5]

    grad_stream = cotangent
    mlp_parts, attn_parts = [None] * layers, [None] * layers
    small_grads = [None] * layers
    over_rows = lambda value: jnp.sum(value.astype(F32), axis=0)
    for l in reversed(range(layers)):
        qkv, out, up, down = weights[l]
        gains = gain_rows[l]
        (
            low,
            projected,
            kept_keys,
            offsets,
            mixture,
            unit_early,
            rate_early,
            mid_low,
            hidden_in,
            hidden_out,
            unit_late,
            rate_late,
        ) = stored[l]
        grad_second = norm_back(grad_stream, unit_late, rate_late, gains[1])
        gain_late, shift_late = over_rows(grad_stream * unit_late), over_rows(grad_stream)
        second_low = grad_second.astype(BF)
        grad_down = [dot_tn(second_low, hidden_out[t]).astype(BF) for t in T]
        grad_pre = [
            (dot(second_low, down[t]) * gelu_slope(hidden_in[t])).astype(BF) for t in T
        ]
        grad_up = [dot_tn(mid_low, grad_pre[t]).astype(BF) for t in T]
        mlp_parts[l] = [jnp.concatenate([grad_up[t], grad_down[t]], axis=1) for t in T]
        grad_mid = grad_second + sum(dot_nt(grad_pre[t], up[t]) for t in T)
        grad_first = norm_back(grad_mid, unit_early, rate_early, gains[0])
        gain_early, shift_early = over_rows(grad_mid * unit_early), over_rows(grad_mid)
        first_low = grad_first.astype(BF)
        grad_out = [dot_tn(first_low, mixture[t]).astype(BF) for t in T]
        grad_proj = []
        for t in T:
            grad_mix = dot(first_low, out[t]).astype(BF)
            dq, dk, dv = attend_back(
                projected[t],
                kept_keys[t],
                kept_keys[t],
                offsets,
                head_cols,
                grad_mix,
                seg_q,
                seg_k,
                F32 if sharers > 1 else BF,
            )
            if sharers > 1:
                dk = lax.psum_scatter(dk, "tlo", scatter_dimension=0, tiled=True).astype(BF)
                dv = lax.psum_scatter(dv, "tlo", scatter_dimension=0, tiled=True).astype(BF)
            grad_proj.append((dq, dk, dv))
        grad_qkv = [
            jnp.concatenate([dot_tn(low, part).astype(BF) for part in grad_proj[t]], axis=1)
            for t in T
        ]
        attn_parts[l] = [jnp.concatenate([grad_qkv[t], grad_out[t]], axis=1) for t in T]
        grad_stream = grad_first + sum(
            dot_nt(grad_proj[t][k], qkv[t][:, k * head_cols : (k + 1) * head_cols])
            for t in T
            for k in range(3)
        )
        small_grads[l] = (
            jnp.stack([gain_early, gain_late]),
            jnp.stack(
                [
                    jnp.concatenate([over_rows(grad_proj[t][0]) for t in T]),
                    jnp.concatenate([over_rows(grad_proj[t][2]) for t in T]),
                    over_rows(grad_first),
                    shift_early,
                    over_rows(grad_second),
                    shift_late,
                ]
            ),
            jnp.concatenate([over_rows(grad_pre[t]) for t in T]),
        )
    mlp_done, attn_done = [None] * layers, [None] * layers
    for l in reversed(range(layers)):
        mlp_done[l] = scatter_grads(mlp_parts[l])
        attn_done[l] = scatter_grads(attn_parts[l])
    fold = lambda whole: jnp.moveaxis(
        whole.reshape(whole.shape[:-1] + (devices, whole.shape[-1] // devices)), -2, 0
    ).reshape(devices, -1)
    stacked = [jnp.stack([small_grads[l][i] for l in range(layers)]) for i in range(3)]
    summed = scatter_small(jnp.concatenate([fold(whole) for whole in stacked], axis=1))
    return (
        stream.astype(BF),
        grad_stream,
        jnp.stack(
            [
                jnp.stack(
                    [attn_done[l][:, k * head_cols : (k + 1) * head_cols] for k in range(3)]
                )
                for l in range(layers)
            ]
        ),
        jnp.stack([attn_done[l][:, 3 * head_cols :].T for l in range(layers)]),
        jnp.stack([mlp_done[l][:, :hidden] for l in range(layers)]),
        jnp.stack([mlp_done[l][:, hidden:].T for l in range(layers)]),
        summed[: cuts[0]].reshape(norm_gains.shape),
        summed[cuts[0] : cuts[1]].reshape(row_biases.shape),
        summed[cuts[1] :].reshape(ff_bias.shape),
    )


def solution(mesh):
    def whole(*args):
        inputs, seg_ids = args[:2]
        depth, blocks = mesh.shape["dp"], mesh.shape["tensor"]
        rows = inputs.shape[0] // (depth * blocks)
        sharers = max(1, seg_ids.shape[1] // rows)
        inner = Mesh(mesh.devices.reshape(depth, blocks // sharers, sharers), RANKS)
        tensor = ("thi", "tlo")
        row_wise = P(RANKS, None)
        weight_specs = (
            P(None, None, "dp", tensor),
            P(None, tensor, "dp"),
            P(None, "dp", tensor),
            P(None, tensor, "dp"),
            P(None, None, RANKS),
            P(None, None, RANKS),
            P(None, RANKS),
        )
        return jax.shard_map(
            on_device,
            mesh=inner,
            in_specs=(row_wise, P("dp", None)) + weight_specs + (row_wise,),
            out_specs=(row_wise, row_wise) + weight_specs,
            check_vma=False,
        )(*args)

    return whole
```

```python
from functools import partial

import jax
import jax.numpy as jnp
import numpy as np
from jax import lax
from jax.experimental import pallas as pl
from jax.experimental.pallas import tpu as pltpu
from jax.sharding import Mesh
from jax.sharding import PartitionSpec as P

HD = 64
EPSILON = 1e-06
HALF_ROOT = 0.7071067811865476
INV_ROOT_TAU = 0.3989422804014327
BF = jnp.bfloat16
F32 = jnp.float32
RANKS = ("dp", "thi", "tlo")
SPREAD = ("thi", "tlo", "dp")


def norm_parts(summed):
    centre = summed - jnp.mean(summed, axis=-1, keepdims=True)
    spread = jnp.mean(centre * centre, axis=-1, keepdims=True)
    rate = lax.rsqrt(spread + EPSILON)
    return centre * rate, rate


def norm_back(grad, unit, rate, gain):
    scaled = grad * gain
    return rate * (
        scaled
        - jnp.mean(scaled, axis=-1, keepdims=True)
        - unit * jnp.mean(scaled * unit, axis=-1, keepdims=True)
    )


def dot(a, b):
    return jnp.dot(a, b, preferred_element_type=F32)


def dot_nt(a, b):
    return lax.dot_general(a, b, (((1,), (1,)), ((), ())), preferred_element_type=F32)


def dot_tn(a, b):
    return lax.dot_general(a, b, (((0,), (0,)), ((), ())), preferred_element_type=F32)


def attend_kernel(q_ref, k_ref, v_ref, segq_ref, segk_ref, out_ref):
    same = segk_ref[0] == segq_ref[0]
    outs = []
    for half in range(q_ref.shape[1] // HD):
        cols = slice(half * HD, half * HD + HD)
        q = (q_ref[:, cols].astype(F32) * HD ** (-0.5)).astype(BF)
        scores = jnp.where(same, dot_nt(k_ref[:, cols], q), -jnp.inf)
        top = jnp.max(scores, axis=0, keepdims=True)
        weights = jnp.exp(scores - top)
        total = jnp.sum(weights, axis=0, keepdims=True)
        probs = (weights * (1.0 / total)).astype(BF)
        outs.append(dot_tn(probs, v_ref[:, cols]))
    out_ref[...] = jnp.concatenate(outs, axis=1).astype(BF)


def attend_back_kernel(q_ref, k_ref, v_ref, grad_ref, segq_ref, segk_ref, *out_refs):
    same = segk_ref[0] == segq_ref[0]
    found = [], [], []
    for half in range(q_ref.shape[1] // HD):
        cols = slice(half * HD, half * HD + HD)
        q = (q_ref[:, cols].astype(F32) * HD ** (-0.5)).astype(BF)
        k, v, grad = k_ref[:, cols], v_ref[:, cols], grad_ref[:, cols]
        scores = jnp.where(same, dot_nt(k, q), -jnp.inf)
        top = jnp.max(scores, axis=0, keepdims=True)
        weights = jnp.exp(scores - top)
        probs = weights * (1.0 / jnp.sum(weights, axis=0, keepdims=True))
        grad_probs = dot_nt(v, grad)
        inner = jnp.sum(grad_probs * probs, axis=0, keepdims=True)
        grad_scores = (probs * (grad_probs - inner)).astype(BF)
        found[0].append(dot_tn(grad_scores, k) * HD ** (-0.5))
        found[1].append(dot(grad_scores, q))
        found[2].append(dot(probs.astype(BF), grad))
    for i in range(3):
        target = out_refs[0].at[i] if len(out_refs) == 1 else out_refs[i]
        target[...] = jnp.concatenate(found[i], axis=1).astype(target.dtype)


def attention_specs(rows, keys, cols):
    wide = 128 if cols % 128 == 0 else cols
    pairs = cols // wide
    part = lambda n, k: pl.BlockSpec(
        (n, wide), lambda s, j: (s, (j // pairs * 3 + k) * pairs + j % pairs)
    )
    plain = lambda n: pl.BlockSpec((n, wide), lambda s, j: (s, j))
    segs = [
        pl.BlockSpec((1, 1, rows), lambda s, j: (s, 0, 0)),
        pl.BlockSpec((1, keys, 1), lambda s, j: (s, 0, 0)),
    ]
    return wide, pairs, [part(rows, 0), part(keys, 1), part(keys, 2)], plain, segs


def attend(q, kv, cols, seg_q, seg_k):
    sets, parts = seg_q.shape[0], q.shape[1] // (3 * cols)
    rows, keys = q.shape[0] // sets, kv.shape[0] // sets
    _, pairs, specs, plain, segs = attention_specs(rows, keys, cols)
    work = parts * cols // HD * sets * rows * keys
    return pl.pallas_call(
        attend_kernel,
        grid=(sets, parts * pairs),
        in_specs=specs + segs,
        out_specs=plain(rows),
        out_shape=jax.ShapeDtypeStruct((q.shape[0], parts * cols), BF),
        cost_estimate=pl.CostEstimate(
            flops=16 * work * HD, bytes_accessed=2 * q.size * 2, transcendentals=work
        ),
        name="attend",
    )(q, kv, kv, seg_q[:, None, :], seg_k[:, :, None])


def attend_back(q, kv, cols, grad, seg_q, seg_k):
    sets, parts = seg_q.shape[0], q.shape[1] // (3 * cols)
    rows, keys = q.shape[0] // sets, kv.shape[0] // sets
    wide, pairs, specs, plain, segs = attention_specs(rows, keys, cols)
    work = parts * cols // HD * sets * rows * keys
    if rows == keys:
        out_specs = pl.BlockSpec((3, rows, wide), lambda s, j: (0, s, j))
        out_shape = jax.ShapeDtypeStruct((3, q.shape[0], parts * cols), BF)
    else:
        out_specs = [plain(rows), plain(keys), plain(keys)]
        out_shape = [
            jax.ShapeDtypeStruct((q.shape[0], parts * cols), BF),
            jax.ShapeDtypeStruct((kv.shape[0], parts * cols), F32),
            jax.ShapeDtypeStruct((kv.shape[0], parts * cols), F32),
        ]
    return pl.pallas_call(
        attend_back_kernel,
        grid=(sets, parts * pairs),
        in_specs=specs + [plain(rows)] + segs,
        out_specs=out_specs,
        out_shape=out_shape,
        cost_estimate=pl.CostEstimate(
            flops=40 * work * HD, bytes_accessed=4 * q.size * 2, transcendentals=work
        ),
        name="attend_back",
    )(q, kv, kv, grad, seg_q[:, None, :], seg_k[:, :, None])


def tile(most, *sizes):
    for size in (1024, 768, 512, 384, 256, 128):
        if size <= most and all(n % size == 0 for n in sizes):
            return size
    raise ValueError("width")


def cost(flops, *arrays):
    return pl.CostEstimate(
        flops=flops,
        bytes_accessed=sum(a.size * a.dtype.itemsize for a in arrays),
        transcendentals=0,
    )


def times_weight(which, x, weight, cols, finish, extras, out_types, name):
    rows, parts, count = x.shape[0], len(weight), len(weight[0])
    bn = tile(1024, cols, *[v[3] for w in weight for v in w])
    per = cols // bn

    def spec(t, view):
        _, block, height, first = view
        local = lambda j: first // bn + jnp.clip(j - t * per, 0, per - 1)
        if block is None:
            return pl.BlockSpec((height, bn), lambda j, _: (0, local(j)))
        return pl.BlockSpec((height, bn), lambda j, names: (names[block], local(j)))

    def kernel(which_ref, x_ref, *refs):
        step = pl.program_id(0)
        more = refs[parts * count : parts * count + len(extras)]
        outs = refs[parts * count + len(extras) :]
        for t in range(parts):

            @pl.when((step >= t * per) & (step < t * per + per))
            def _(t=t):
                total, first = None, 0
                for ref in refs[t * count : (t + 1) * count]:
                    height = ref.shape[0]
                    part = dot(x_ref[:, first : first + height], ref[...])
                    total = part if total is None else total + part
                    first += height
                for ref, out in zip(outs, finish(total, *[e[...] for e in more])):
                    ref[...] = out.astype(ref.dtype)

    return pl.pallas_call(
        kernel,
        grid_spec=pltpu.PrefetchScalarGridSpec(
            num_scalar_prefetch=1,
            grid=(parts * per,),
            in_specs=[pl.BlockSpec(x.shape, lambda j, _: (0, 0))]
            + [spec(t, v) for t in range(parts) for v in weight[t]]
            + [pl.BlockSpec((e.shape[0], bn), lambda j, _: (0, j)) for e in extras],
            out_specs=[pl.BlockSpec((rows, bn), lambda j, _: (0, j)) for _ in out_types],
        ),
        out_shape=[jax.ShapeDtypeStruct((rows, parts * cols), t) for t in out_types],
        cost_estimate=cost(2 * x.size * cols * parts, x, x),
        name=name,
    )(which, x, *[v[0] for w in weight for v in w], *extras)


def times_transposed(which, right, weight, name):
    parts = len(weight)
    stack, rows, each = right.shape[0], right.shape[1], right.shape[2] // parts
    bn = tile(1024, each, *[v[3] for w in weight for v in w])
    per = each // bn
    heights = [v[2] for v in weight[0]]
    width = sum(heights)

    def spec(view):
        _, block, height, first = view
        if block is None:
            return pl.BlockSpec((height, bn), lambda j, _: (0, first // bn + j))
        return pl.BlockSpec((height, bn), lambda j, names: (names[block], first // bn + j))

    def kernel(which_ref, *refs):
        out_ref = refs[-1]
        begin = pl.program_id(0) == 0
        place = 0
        for b, height in enumerate(heights):
            cols = slice(place, place + height)
            total = sum(
                dot_nt(refs[t][...], refs[parts + t * len(heights) + b][...])
                for t in range(parts)
            )
            if stack * per == 1:
                out_ref[:, cols] = total
            else:

                @pl.when(begin)
                def _():
                    out_ref[:, cols] = total

                @pl.when(jnp.logical_not(begin))
                def _():
                    out_ref[:, cols] += total

            place += height

    return pl.pallas_call(
        kernel,
        grid_spec=pltpu.PrefetchScalarGridSpec(
            num_scalar_prefetch=1,
            grid=(stack * per,),
            in_specs=[
                pl.BlockSpec(
                    (None, rows, bn), lambda j, _, t=t: (j // per, 0, t * per + j % per)
                )
                for t in range(parts)
            ]
            + [spec(v) for w in weight for v in w],
            out_specs=pl.BlockSpec((rows, width), lambda j, _: (0, 0)),
        ),
        out_shape=jax.ShapeDtypeStruct((rows, width), F32),
        cost_estimate=cost(2 * rows * width * stack * each * parts, right),
        name=name,
    )(which, *[right] * parts, *[v[0] for w in weight for v in w])


def weight_grads(pairs, parts, section, sections, add=None, blocks=1, name="weight_grads"):
    rows, width = pairs[0][0].shape
    height = width // sections
    bn = tile(1024, *[right.shape[2] // parts for _, right in pairs])
    counts = [right.shape[0] * right.shape[2] // parts // bn for _, right in pairs]
    starts = [sum(counts[:i]) for i in range(len(pairs))]
    columns = sum(counts) * bn
    low = height // blocks

    def kernel(*refs):
        step = pl.program_id(0)
        turned = refs[-len(pairs) :]
        at = len(pairs) * (1 + parts)
        add_ref = refs[at] if add is not None else None
        outs = refs[at + (add is not None) : -len(pairs)]
        for i in range(len(pairs)):
            base = i * (1 + parts)

            @pl.when(step == starts[i])
            def _(i=i, base=base):
                turned[i][...] = refs[base][...].T

            @pl.when((step >= starts[i]) & (step < starts[i] + counts[i]))
            def _(i=i, base=base):
                for t in range(parts):
                    value = dot(turned[i][...], refs[base + 1 + t][...])
                    if add_ref is not None:
                        value += add_ref[t].astype(F32)
                    value = value.astype(BF)
                    if blocks == 1:
                        outs[0][t] = value
                    else:
                        for b in range(blocks):
                            outs[b * parts + t][...] = value[b * low : (b + 1) * low]

    in_specs, operands = [], []
    for i, (left, right) in enumerate(pairs):
        in_specs.append(pl.BlockSpec((rows, height), lambda j: (0, section)))
        operands.append(left)
        per = right.shape[2] // parts // bn
        for t in range(parts):

            def where(j, i=i, t=t, per=per):
                local = jnp.clip(j - starts[i], 0, counts[i] - 1)
                return local // per, 0, t * per + local % per

            in_specs.append(pl.BlockSpec((None, rows, bn), where))
            operands.append(right)
    if add is not None:
        in_specs.append(pl.BlockSpec((parts, height, bn), lambda j: (0, 0, j)))
        operands.append(add)
    if blocks == 1:
        out_specs = pl.BlockSpec((parts, height, bn), lambda j: (0, 0, j))
        out_shape = jax.ShapeDtypeStruct((parts, height, columns), BF)
    else:
        out_specs = [pl.BlockSpec((low, bn), lambda j: (0, j))] * (blocks * parts)
        out_shape = [jax.ShapeDtypeStruct((low, columns), BF)] * (blocks * parts)
    found = pl.pallas_call(
        kernel,
        grid=(sum(counts),),
        in_specs=in_specs,
        out_specs=out_specs,
        out_shape=out_shape,
        scratch_shapes=[pltpu.VMEM((height, rows), BF) for _ in pairs],
        cost_estimate=cost(2 * height * rows * columns * parts, *[p[1] for p in pairs]),
        name=name,
    )(*operands)
    if blocks == 1:
        return found
    return [[found[b * parts + t] for t in range(parts)] for b in range(blocks)]


def three_parts(value):
    first = lax.reduce_precision(value, 8, 7)
    second = lax.reduce_precision(value - first, 8, 7)
    return [part.astype(BF) for part in (first, second, value - first - second)]


def pack_small(row, height):
    flat = jnp.concatenate(three_parts(row))
    columns = -(-flat.shape[0] // (128 * height)) * 128
    return jnp.pad(flat, (0, height * columns - flat.shape[0])).reshape(height, columns)


def unpack_small(packed, size, height):
    depth = lax.axis_size("dp")
    flat = packed.reshape(-1, depth, height * packed.shape[1])[:, :, : 3 * size]
    parts = jnp.sum(flat.reshape(-1, depth, 3, size).astype(F32), axis=2)
    return jnp.swapaxes(parts, 0, 1).reshape(-1, size)


def swap(value, mask):
    count = lax.axis_size("dp") * lax.axis_size("thi") * lax.axis_size("tlo")
    return lax.ppermute(value, RANKS, [(i, i ^ mask) for i in range(count)])


def relative_small(parts):
    return jnp.take(parts, jnp.arange(parts.shape[0]) ^ lax.axis_index(RANKS), axis=0)


def scatter_small(held, until):
    mask = held.shape[0] // 2
    while mask >= until:
        held = held[:mask] + swap(held[mask:], mask)
        mask //= 2
    return held


def over_dp(value, mask):
    count = lax.axis_size("dp")
    return lax.ppermute(value, "dp", [(i, i ^ mask) for i in range(count)])


def over_tensor(value, mask):
    count = lax.axis_size("thi") * lax.axis_size("tlo")
    return lax.ppermute(value, ("thi", "tlo"), [(i, i ^ mask) for i in range(count)])


def tensor_size():
    return lax.axis_size("thi") * lax.axis_size("tlo")


def hold(*trees):
    return lax.optimization_barrier(trees)


def gather_far(shard):
    rest = lax.axis_size("dp") // 4
    return jnp.concatenate([shard] + [over_dp(shard, 4 * m) for m in range(1, rest)], axis=0)


def gather_sides(own):
    return over_dp(own, 2), [over_tensor(own, m) for m in range(1, tensor_size())]


def gather_corners(own, sides):
    across, near = sides
    half = own.shape[0] // 2
    far = [
        jnp.concatenate([over_dp(block[:half], 2), over_tensor(across[half:], m + 1)], axis=0)
        for m, block in enumerate(near)
    ]
    return [[own] + near, [across] + far]


def gather_core(here):
    return [here, [[over_dp(block, 1) for block in line] for line in here]]


def block_views(blocks, first):
    return [
        [(line[t], None, line[t].shape[0], first) for half in blocks for line in half]
        for t in range(len(blocks[0][0]))
    ]


def wide(value):
    return value.astype(F32)


def scatter_corners(line):
    half = line[0][0].shape[0] // 2
    return (
        [over_dp(block[:half], 2) for block in line[1][1:]],
        [over_tensor(block[half:], m + 1) for m, block in enumerate(line[1][1:])],
    )


def scatter_sides(line, corners):
    near, across = line[0][1:], line[1][0]
    half = across.shape[0] // 2
    tops, bottoms = corners
    near = [
        jnp.concatenate([(wide(a[:half]) + wide(b)).astype(BF), a[half:]], axis=0)
        for a, b in zip(near, tops)
    ]
    if bottoms:
        low = (wide(across[half:]) + sum(wide(b) for b in bottoms)).astype(BF)
        across = jnp.concatenate([across[:half], low], axis=0)
    return [over_dp(across, 2)] + [over_tensor(block, m + 1) for m, block in enumerate(near)]


def scatter_far(line, sides):
    own = line[0][0]
    rest = lax.axis_size("dp") // 4
    height = own.shape[0] // rest
    piece = lambda m: sum(
        (wide(v[m * height : (m + 1) * height]) for v in sides),
        wide(own[m * height : (m + 1) * height]),
    )
    return [piece(0)] + [over_dp(piece(m).astype(BF), 4 * m) for m in range(1, rest)]


def scatter_end(addends):
    return sum(wide(v) for v in addends)


def relative_blocks():
    depth = lax.axis_size("dp")
    rest = depth // 4
    own = lax.axis_index("dp")
    place = np.arange(depth)
    core, second, far = place // (2 * rest), place // rest % 2, place % rest
    order = jnp.asarray(far * 4 + second * 2 + core) ^ own
    mask = jnp.arange(depth) ^ own
    places = ((mask & 1) * 2 + (mask >> 1 & 1)) * rest + (mask >> 2)
    return order, places


def reorder(rows, order):
    cut = rows.reshape(rows.shape[:-1] + (order.shape[0], -1))
    return jnp.take(cut, order, axis=-2).reshape(rows.shape)


def selection(order, width):
    each = width // order.shape[0]
    source = (order[:, None] * each + jnp.arange(each)[None]).reshape(-1)
    return (jnp.arange(width)[:, None] == source[None, :]).astype(BF)


def select_wide(rows, chooser):
    return sum(dot(part, chooser) for part in three_parts(rows))


def on_device(
    inputs,
    seg_ids,
    qkv_weight,
    out_weight,
    up_weight,
    down_weight,
    norm_gains,
    row_biases,
    ff_bias,
    cotangent,
):
    blocks = tensor_size()
    sharers = lax.axis_size("tlo")
    rows, width = inputs.shape
    layers = qkv_weight.shape[0]
    head_cols = qkv_weight.shape[3]
    hidden = up_weight.shape[2]
    length = seg_ids.shape[1]
    sets = max(1, rows // length)
    T = range(blocks)

    seg_k = lax.dynamic_slice_in_dim(seg_ids, lax.axis_index("thi") * sets, sets)
    seg_q = seg_k
    if sharers > 1:
        seg_q = lax.dynamic_slice_in_dim(seg_k, lax.axis_index("tlo") * rows, rows, axis=1)

    order, places = relative_blocks()
    pick, unpick = selection(order, width), selection(places, width)
    own_t = lax.axis_index(("thi", "tlo"))
    same_t = jnp.arange(blocks, dtype=jnp.int32)
    relative_t = (same_t ^ own_t).astype(jnp.int32)

    join = lambda *parts: jnp.concatenate(parts, axis=1).astype(BF)
    qkv_of = lambda l: [qkv_weight[l, k] for k in range(3)]
    spread = lambda shard: lax.all_gather(shard, SPREAD, axis=0, tiled=True)
    views = lambda whole, first: [[(whole, t, width, first)] for t in T]
    row = jnp.concatenate([norm_gains.reshape(-1), row_biases.reshape(-1), ff_bias.reshape(-1)])
    height = qkv_weight.shape[2]
    first_whole = spread(jnp.concatenate([join(*qkv_of(0)), pack_small(row, height)], axis=1))
    small = unpack_small(first_whole[:, 3 * head_cols :], row.shape[0], height)
    mlp_views = [None] * layers
    for l in range(1, layers):
        mlp = spread(join(up_weight[l], down_weight[l].T))
        mlp_views[l] = views(mlp, 0), views(mlp, hidden)
    mid_own = gather_far(join(up_weight[0], out_weight[0].T))
    down_shard = join(down_weight[0].T)
    mid_own, down_shard = hold(mid_own, down_shard)
    mid_sides = gather_sides(mid_own)
    down_own = gather_far(down_shard)
    mid_here = gather_corners(mid_own, mid_sides)
    mid_blocks = gather_core(mid_here)
    down_own, mid_here = hold(down_own, mid_here)
    down_sides = gather_sides(down_own)
    later_shards = [join(*qkv_of(l), out_weight[l].T) for l in range(1, layers)]

    devices = small.shape[0]
    cuts = np.cumsum([norm_gains.size, row_biases.size])
    spread_out = lambda piece, like: jnp.moveaxis(
        piece.reshape((devices,) + like.shape), 0, -2
    ).reshape(like.shape[:-1] + (devices * like.shape[-1],))
    gain_rows = spread_out(small[:, : cuts[0]], norm_gains)
    shift_rows = spread_out(small[:, cuts[0] : cuts[1]], row_biases)
    up_shifts = spread_out(small[:, cuts[1] :], ff_bias)

    def vectors(l):
        gains, shifts, up_shift = gain_rows[l], shift_rows[l], up_shifts[l]
        heads, wide = reorder(shifts[:2], relative_t), shifts[2:]
        if l == 0:
            gains, wide = reorder(gains, order), reorder(wide, order)
            up_shift = reorder(up_shift, relative_t)
        else:
            gains = jnp.concatenate([reorder(gains[:1], order), gains[1:]])
            wide = jnp.concatenate([reorder(wide[:2], order), wide[2:]])
        heads = heads.reshape(2, blocks, head_cols)
        qkv_shift = jnp.stack([heads[0], jnp.zeros_like(heads[0]), heads[1]], axis=1)
        return gains, qkv_shift.reshape(1, -1), wide, up_shift[None]

    add_shift = lambda value, shift: (value + shift,)

    def enter(value, shift):
        value = value + shift
        upto = 0.5 * (1.0 + lax.erf(value * HALF_ROOT))
        return value * upto, upto + value * jnp.exp(-0.5 * value * value) * INV_ROOT_TAU

    def leave(value, slope):
        return (value * slope.astype(F32),)

    gather_keys = (
        (lambda v: lax.all_gather(v, "tlo", axis=0, tiled=True)) if sharers > 1 else (lambda v: v)
    )
    stored = []
    stream = dot(inputs, pick)
    for l in range(layers):
        gains, qkv_shift, shifts, up_shift = vectors(l)
        if l > 1:
            stream = select_wide(stream, pick)
        if l == 0:
            qkv, low = views(first_whole, 0), inputs
        else:
            qkv, out = attn_views[l]
            up, down = mlp_views[l]
            low = stream.astype(BF)
        (projected,) = times_weight(
            relative_t, low, qkv, 3 * head_cols, add_shift, [qkv_shift], [BF], "project"
        )
        if l == 0:
            projected, down_sides = hold(projected, down_sides)
            down_here = gather_corners(down_own, down_sides)
        keys = gather_keys(projected)
        mixture = attend(projected, keys, head_cols, seg_q, seg_k)
        if l == 0:
            mixture, down_here, later_shards = hold(mixture, down_here, later_shards)
            later_own = [gather_far(s) for s in later_shards]
            up, out = block_views(mid_blocks, 0), block_views(mid_blocks, hidden)
            down = block_views(gather_core(down_here), 0)
        attended = times_transposed(relative_t, mixture[None], out, "attended")
        unit_early, rate_early = norm_parts(stream + (attended + shifts[0]))
        mid = unit_early * gains[0] + shifts[1]
        if l == 0:
            mid, later_own = hold(mid, later_own)
            later_sides = [gather_sides(own) for own in later_own]
        else:
            mid = select_wide(mid, unpick)
        mid_low = mid.astype(BF)
        hidden_out, slopes = times_weight(
            same_t, mid_low, up, hidden, enter, [up_shift], [BF, BF], "enter"
        )
        if l == 0:
            hidden_out, later_sides = hold(hidden_out, later_sides)
            later_here = [gather_corners(o, s) for o, s in zip(later_own, later_sides)]
        branch = times_transposed(same_t, hidden_out[None], down, "branch")
        if l == 0:
            branch, later_here = hold(branch, later_here)
            attn_views = [None]
            for got in [gather_core(here) for here in later_here]:
                attn_views.append((block_views(got, 0), block_views(got, 3 * head_cols)))
        unit_late, rate_late = norm_parts(mid + (branch + shifts[2]))
        stored.append(
            (
                qkv,
                out,
                up,
                down,
                gains,
                low,
                projected,
                keys,
                mixture,
                unit_early,
                rate_early,
                mid_low,
                slopes,
                hidden_out,
                unit_late,
                rate_late,
            )
        )
        stream = unit_late * gains[1] + shifts[3]
    if layers == 1:
        stream = select_wide(stream, unpick)

    grad_stream = cotangent if layers > 1 else select_wide(cotangent, pick)
    mlp_done, attn_done = [None] * layers, [None] * layers
    small_grads = [None] * layers
    over_rows = lambda value: jnp.sum(value.astype(F32), axis=0)
    fold = lambda whole: jnp.moveaxis(
        whole.reshape(whole.shape[:-1] + (devices, whole.shape[-1] // devices)), -2, 0
    ).reshape(devices, -1)
    flying = None
    for l in reversed(range(layers)):
        (
            qkv,
            out,
            up,
            down,
            gains,
            low,
            projected,
            keys,
            mixture,
            unit_early,
            rate_early,
            mid_low,
            slopes,
            hidden_out,
            unit_late,
            rate_late,
        ) = stored[l]
        if 0 < l < layers - 1:
            grad_stream = select_wide(grad_stream, unpick)
        grad_second = norm_back(grad_stream, unit_late, rate_late, gains[1])
        gain_late, shift_late = over_rows(grad_stream * unit_late), over_rows(grad_stream)
        second_low = grad_second.astype(BF)
        (grad_pre,) = times_weight(same_t, second_low, down, hidden, leave, [slopes], [BF], "leave")
        mlp_pairs = [(mid_low, grad_pre[None]), (second_low, hidden_out[None])]
        if l == 0:
            if flying is not None:
                line, corners = flying
                grad_pre, corners = hold(grad_pre, corners)
                sides = scatter_sides(line, corners)
            mlp_send = weight_grads(mlp_pairs, blocks, 1, 2, name="mlp_send")
            mlp_send, grad_pre = hold(mlp_send, grad_pre)
            mlp_came = over_dp(mlp_send, 1)
        else:
            whole = weight_grads(mlp_pairs, blocks, 0, 1, name="mlp_grads")
            whole, grad_pre = hold(whole, grad_pre)
            mlp_done[l] = lax.psum_scatter(
                whole.reshape(-1, whole.shape[2]), SPREAD, scatter_dimension=0, tiled=True
            ).astype(F32)
        grad_mid = grad_second + times_transposed(same_t, grad_pre[None], up, "grad_mid")
        if l > 0:
            grad_mid = select_wide(grad_mid, pick)
        grad_first = norm_back(grad_mid, unit_early, rate_early, gains[0])
        gain_early, shift_early = over_rows(grad_mid * unit_early), over_rows(grad_mid)
        first_low = grad_first.astype(BF)
        if l == 0:
            first_low, mlp_came = hold(first_low, mlp_came)
            mlp_line = weight_grads(
                mlp_pairs, blocks, 0, 2, add=mlp_came, blocks=2, name="mlp_keep"
            )
            if flying is not None:
                first_low, mlp_line, sides = hold(first_low, mlp_line, sides)
                addends = scatter_far(line, sides)
            else:
                first_low, mlp_line = hold(first_low, mlp_line)
            mlp_corners = scatter_corners(mlp_line)
        (grad_mix,) = times_weight(
            relative_t, first_low, out, head_cols, lambda v: (v,), [], [BF], "grad_mix"
        )
        grad_proj = attend_back(projected, keys, head_cols, grad_mix, seg_q, seg_k)
        if sharers > 1:
            grad_proj = jnp.stack(
                [grad_proj[0]]
                + [
                    lax.psum_scatter(v, "tlo", scatter_dimension=0, tiled=True).astype(BF)
                    for v in grad_proj[1:]
                ]
            )
        left = dot(low, pick).astype(BF) if l == 0 else low
        attn_pairs = [(left, grad_proj), (first_low, mixture[None])]
        attn_send = weight_grads(attn_pairs, blocks, 1, 2, name="attn_send")
        if l == 0:
            if flying is not None:
                attn_send, addends = hold(attn_send, addends)
                attn_done[l + 1] = scatter_end(addends)
            attn_send, grad_proj, mlp_corners = hold(attn_send, grad_proj, mlp_corners)
            mlp_sides = scatter_sides(mlp_line, mlp_corners)
        else:
            attn_send, grad_proj = hold(attn_send, grad_proj)
        attn_came = over_dp(attn_send, 1)
        back = times_transposed(relative_t, grad_proj, qkv, "grad_stream")
        back, attn_came = hold(back, attn_came)
        attn_line = weight_grads(
            attn_pairs, blocks, 0, 2, add=attn_came, blocks=2, name="attn_keep"
        )
        heads_grad = jnp.stack([over_rows(grad_proj[0]), over_rows(grad_proj[2])])
        wide_grad = jnp.stack(
            [over_rows(grad_first), shift_early, over_rows(grad_second), shift_late]
        )
        gains_grad = jnp.stack([gain_early, gain_late])
        ups_grad = over_rows(grad_pre)
        heads_grad = reorder(heads_grad, relative_t)
        if l == 0:
            ups_grad = reorder(ups_grad, relative_t)
            wide_grad, gains_grad = reorder(wide_grad, places), reorder(gains_grad, places)
        else:
            wide_grad = jnp.concatenate([reorder(wide_grad[:2], places), wide_grad[2:]])
            gains_grad = jnp.concatenate([reorder(gains_grad[:1], places), gains_grad[1:]])
        small_grads[l] = gains_grad, jnp.concatenate([heads_grad, wide_grad]), ups_grad
        if l == 0:
            smalls = [jnp.stack([small_grads[n][i] for n in range(layers)]) for i in range(3)]
            small_sums = relative_small(
                jnp.concatenate([fold(whole) for whole in smalls], axis=1)
            )
            attn_line, mlp_sides, back, small_sums = hold(attn_line, mlp_sides, back, small_sums)
            mlp_addends = scatter_far(mlp_line, mlp_sides)
            attn_corners = scatter_corners(attn_line)
            attn_corners, mlp_addends = hold(attn_corners, mlp_addends)
            attn_sides = scatter_sides(attn_line, attn_corners)
            small_sums = scatter_small(small_sums, 2 * blocks)
            attn_sides, small_sums = hold(attn_sides, small_sums)
            attn_done[l] = scatter_end(scatter_far(attn_line, attn_sides))
            mlp_done[l] = scatter_end(mlp_addends)
            summed = scatter_small(small_sums, 1)[0]
            input_grad = select_wide(grad_first, unpick) + back
        else:
            attn_line, back = hold(attn_line, back)
            flying = attn_line, scatter_corners(attn_line)
            grad_stream = grad_first + back

    return (
        stream.astype(BF),
        input_grad,
        jnp.stack(
            [
                jnp.stack(
                    [attn_done[l][:, k * head_cols : (k + 1) * head_cols] for k in range(3)]
                )
                for l in range(layers)
            ]
        ),
        jnp.stack([attn_done[l][:, 3 * head_cols :].T for l in range(layers)]),
        jnp.stack([mlp_done[l][:, :hidden] for l in range(layers)]),
        jnp.stack([mlp_done[l][:, hidden:].T for l in range(layers)]),
        summed[: cuts[0]].reshape(norm_gains.shape),
        summed[cuts[0] : cuts[1]].reshape(row_biases.shape),
        summed[cuts[1] :].reshape(ff_bias.shape),
    )


def solution(mesh):
    def whole(*args):
        inputs, seg_ids = args[:2]
        depth, blocks = mesh.shape["dp"], mesh.shape["tensor"]
        rows = inputs.shape[0] // (depth * blocks)
        sharers = max(1, seg_ids.shape[1] // rows)
        inner = Mesh(mesh.devices.reshape(depth, blocks // sharers, sharers), RANKS)
        tensor = ("thi", "tlo")
        row_wise = P(RANKS, None)
        weight_specs = (
            P(None, None, "dp", tensor),
            P(None, tensor, "dp"),
            P(None, "dp", tensor),
            P(None, tensor, "dp"),
            P(None, None, RANKS),
            P(None, None, RANKS),
            P(None, RANKS),
        )
        return jax.shard_map(
            on_device,
            mesh=inner,
            in_specs=(row_wise, P("dp", None)) + weight_specs + (row_wise,),
            out_specs=(row_wise, row_wise) + weight_specs,
            check_vma=False,
        )(*args)

    return whole
```

```python
from functools import partial

import jax
import jax.numpy as jnp
import numpy as np
from jax import lax
from jax.experimental import pallas as pl
from jax.experimental.pallas import tpu as pltpu
from jax.sharding import Mesh
from jax.sharding import PartitionSpec as P

HD = 64
EPSILON = 1e-06
HALF_ROOT = 0.7071067811865476
INV_ROOT_TAU = 0.3989422804014327
BF = jnp.bfloat16
F32 = jnp.float32
RANKS = ("dp", "thi", "tlo")
SPREAD = ("thi", "tlo", "dp")


def norm_parts(summed):
    centre = summed - jnp.mean(summed, axis=-1, keepdims=True)
    spread = jnp.mean(centre * centre, axis=-1, keepdims=True)
    rate = lax.rsqrt(spread + EPSILON)
    return centre * rate, rate


def norm_back(grad, unit, rate, gain):
    scaled = grad * gain
    return rate * (
        scaled
        - jnp.mean(scaled, axis=-1, keepdims=True)
        - unit * jnp.mean(scaled * unit, axis=-1, keepdims=True)
    )


def dot(a, b):
    return jnp.dot(a, b, preferred_element_type=F32)


def dot_nt(a, b):
    return lax.dot_general(a, b, (((1,), (1,)), ((), ())), preferred_element_type=F32)


def dot_tn(a, b):
    return lax.dot_general(a, b, (((0,), (0,)), ((), ())), preferred_element_type=F32)


def attend_kernel(q_ref, k_ref, v_ref, segq_ref, segk_ref, out_ref):
    same = segk_ref[0] == segq_ref[0]
    outs = []
    for half in range(q_ref.shape[1] // HD):
        cols = slice(half * HD, half * HD + HD)
        q = (q_ref[:, cols].astype(F32) * HD ** (-0.5)).astype(BF)
        scores = jnp.where(same, dot_nt(k_ref[:, cols], q), -jnp.inf)
        top = jnp.max(scores, axis=0, keepdims=True)
        weights = jnp.exp(scores - top)
        total = jnp.sum(weights, axis=0, keepdims=True)
        probs = (weights * (1.0 / total)).astype(BF)
        outs.append(dot_tn(probs, v_ref[:, cols]))
    out_ref[...] = jnp.concatenate(outs, axis=1).astype(BF)


def attend_back_kernel(q_ref, k_ref, v_ref, grad_ref, segq_ref, segk_ref, *out_refs):
    same = segk_ref[0] == segq_ref[0]
    found = [], [], []
    for half in range(q_ref.shape[1] // HD):
        cols = slice(half * HD, half * HD + HD)
        q = (q_ref[:, cols].astype(F32) * HD ** (-0.5)).astype(BF)
        k, v, grad = k_ref[:, cols], v_ref[:, cols], grad_ref[:, cols]
        scores = jnp.where(same, dot_nt(k, q), -jnp.inf)
        top = jnp.max(scores, axis=0, keepdims=True)
        weights = jnp.exp(scores - top)
        probs = weights * (1.0 / jnp.sum(weights, axis=0, keepdims=True))
        grad_probs = dot_nt(v, grad)
        inner = jnp.sum(grad_probs * probs, axis=0, keepdims=True)
        grad_scores = (probs * (grad_probs - inner)).astype(BF)
        found[0].append(dot_tn(grad_scores, k) * HD ** (-0.5))
        found[1].append(dot(grad_scores, q))
        found[2].append(dot(probs.astype(BF), grad))
    for i in range(3):
        target = out_refs[0].at[i] if len(out_refs) == 1 else out_refs[i]
        target[...] = jnp.concatenate(found[i], axis=1).astype(target.dtype)


def attention_specs(rows, keys, cols):
    wide = 128 if cols % 128 == 0 else cols
    pairs = cols // wide
    part = lambda n, k: pl.BlockSpec(
        (n, wide), lambda s, j: (s, (j // pairs * 3 + k) * pairs + j % pairs)
    )
    plain = lambda n: pl.BlockSpec((n, wide), lambda s, j: (s, j))
    segs = [
        pl.BlockSpec((1, 1, rows), lambda s, j: (s, 0, 0)),
        pl.BlockSpec((1, keys, 1), lambda s, j: (s, 0, 0)),
    ]
    return wide, pairs, [part(rows, 0), part(keys, 1), part(keys, 2)], plain, segs


def attend(q, kv, cols, seg_q, seg_k):
    sets, parts = seg_q.shape[0], q.shape[1] // (3 * cols)
    rows, keys = q.shape[0] // sets, kv.shape[0] // sets
    _, pairs, specs, plain, segs = attention_specs(rows, keys, cols)
    work = parts * cols // HD * sets * rows * keys
    return pl.pallas_call(
        attend_kernel,
        grid=(sets, parts * pairs),
        in_specs=specs + segs,
        out_specs=plain(rows),
        out_shape=jax.ShapeDtypeStruct((q.shape[0], parts * cols), BF),
        cost_estimate=pl.CostEstimate(
            flops=16 * work * HD, bytes_accessed=2 * q.size * 2, transcendentals=work
        ),
        name="attend",
    )(q, kv, kv, seg_q[:, None, :], seg_k[:, :, None])


def attend_back(q, kv, cols, grad, seg_q, seg_k):
    sets, parts = seg_q.shape[0], q.shape[1] // (3 * cols)
    rows, keys = q.shape[0] // sets, kv.shape[0] // sets
    wide, pairs, specs, plain, segs = attention_specs(rows, keys, cols)
    work = parts * cols // HD * sets * rows * keys
    if rows == keys:
        out_specs = pl.BlockSpec((3, rows, wide), lambda s, j: (0, s, j))
        out_shape = jax.ShapeDtypeStruct((3, q.shape[0], parts * cols), BF)
    else:
        out_specs = [plain(rows), plain(keys), plain(keys)]
        out_shape = [
            jax.ShapeDtypeStruct((q.shape[0], parts * cols), BF),
            jax.ShapeDtypeStruct((kv.shape[0], parts * cols), F32),
            jax.ShapeDtypeStruct((kv.shape[0], parts * cols), F32),
        ]
    return pl.pallas_call(
        attend_back_kernel,
        grid=(sets, parts * pairs),
        in_specs=specs + [plain(rows)] + segs,
        out_specs=out_specs,
        out_shape=out_shape,
        cost_estimate=pl.CostEstimate(
            flops=5 * work * HD, bytes_accessed=q.size, transcendentals=work // 8
        ),
        name="attend_back",
    )(q, kv, kv, grad, seg_q[:, None, :], seg_k[:, :, None])


def tile(most, *sizes):
    for size in (1024, 768, 512, 384, 256, 128):
        if size <= most and all(n % size == 0 for n in sizes):
            return size
    raise ValueError("width")


def cost(name, flops, *arrays):
    short = 1 if name in ("project", "attended", "enter", "branch") else 8
    return pl.CostEstimate(
        flops=flops // short,
        bytes_accessed=sum(a.size * a.dtype.itemsize for a in arrays) // short,
        transcendentals=0,
    )


def times_weight(which, x, weight, cols, finish, extras, out_types, name):
    rows, parts, count = x.shape[0], len(weight), len(weight[0])
    bn = tile(1024, cols, *[v[3] for w in weight for v in w])
    per = cols // bn

    def spec(t, view):
        _, block, height, first = view
        local = lambda j: first // bn + jnp.clip(j - t * per, 0, per - 1)
        if block is None:
            return pl.BlockSpec((height, bn), lambda j, _: (0, local(j)))
        return pl.BlockSpec((height, bn), lambda j, names: (names[block], local(j)))

    def kernel(which_ref, x_ref, *refs):
        step = pl.program_id(0)
        more = refs[parts * count : parts * count + len(extras)]
        outs = refs[parts * count + len(extras) :]
        for t in range(parts):

            @pl.when((step >= t * per) & (step < t * per + per))
            def _(t=t):
                total, first = None, 0
                for ref in refs[t * count : (t + 1) * count]:
                    height = ref.shape[0]
                    part = dot(x_ref[:, first : first + height], ref[...])
                    total = part if total is None else total + part
                    first += height
                for ref, out in zip(outs, finish(total, *[e[...] for e in more])):
                    ref[...] = out.astype(ref.dtype)

    return pl.pallas_call(
        kernel,
        grid_spec=pltpu.PrefetchScalarGridSpec(
            num_scalar_prefetch=1,
            grid=(parts * per,),
            in_specs=[pl.BlockSpec(x.shape, lambda j, _: (0, 0))]
            + [spec(t, v) for t in range(parts) for v in weight[t]]
            + [pl.BlockSpec((e.shape[0], bn), lambda j, _: (0, j)) for e in extras],
            out_specs=[pl.BlockSpec((rows, bn), lambda j, _: (0, j)) for _ in out_types],
        ),
        out_shape=[jax.ShapeDtypeStruct((rows, parts * cols), t) for t in out_types],
        cost_estimate=cost(name, 2 * x.size * cols * parts, x, x),
        name=name,
    )(which, x, *[v[0] for w in weight for v in w], *extras)


def times_transposed(which, right, weight, name):
    parts = len(weight)
    stack, rows, each = right.shape[0], right.shape[1], right.shape[2] // parts
    bn = tile(1024, each, *[v[3] for w in weight for v in w])
    per = each // bn
    heights = [v[2] for v in weight[0]]
    width = sum(heights)

    def spec(view):
        _, block, height, first = view
        if block is None:
            return pl.BlockSpec((height, bn), lambda j, _: (0, first // bn + j))
        return pl.BlockSpec((height, bn), lambda j, names: (names[block], first // bn + j))

    def kernel(which_ref, *refs):
        out_ref = refs[-1]
        begin = pl.program_id(0) == 0
        place = 0
        for b, height in enumerate(heights):
            cols = slice(place, place + height)
            total = sum(
                dot_nt(refs[t][...], refs[parts + t * len(heights) + b][...])
                for t in range(parts)
            )
            if stack * per == 1:
                out_ref[:, cols] = total
            else:

                @pl.when(begin)
                def _():
                    out_ref[:, cols] = total

                @pl.when(jnp.logical_not(begin))
                def _():
                    out_ref[:, cols] += total

            place += height

    return pl.pallas_call(
        kernel,
        grid_spec=pltpu.PrefetchScalarGridSpec(
            num_scalar_prefetch=1,
            grid=(stack * per,),
            in_specs=[
                pl.BlockSpec(
                    (None, rows, bn), lambda j, _, t=t: (j // per, 0, t * per + j % per)
                )
                for t in range(parts)
            ]
            + [spec(v) for w in weight for v in w],
            out_specs=pl.BlockSpec((rows, width), lambda j, _: (0, 0)),
        ),
        out_shape=jax.ShapeDtypeStruct((rows, width), F32),
        cost_estimate=cost(name, 2 * rows * width * stack * each * parts, right),
        name=name,
    )(which, *[right] * parts, *[v[0] for w in weight for v in w])


def weight_grads(pairs, parts, section, sections, add=None, blocks=1, name="weight_grads"):
    rows, width = pairs[0][0].shape
    height = width // sections
    bn = tile(1024, *[right.shape[2] // parts for _, right in pairs])
    counts = [right.shape[0] * right.shape[2] // parts // bn for _, right in pairs]
    starts = [sum(counts[:i]) for i in range(len(pairs))]
    columns = sum(counts) * bn
    low = height // blocks

    def kernel(*refs):
        step = pl.program_id(0)
        turned = refs[-len(pairs) :]
        at = len(pairs) * (1 + parts)
        add_ref = refs[at] if add is not None else None
        outs = refs[at + (add is not None) : -len(pairs)]
        for i in range(len(pairs)):
            base = i * (1 + parts)

            @pl.when(step == starts[i])
            def _(i=i, base=base):
                turned[i][...] = refs[base][...].T

            @pl.when((step >= starts[i]) & (step < starts[i] + counts[i]))
            def _(i=i, base=base):
                for t in range(parts):
                    value = dot(turned[i][...], refs[base + 1 + t][...])
                    if add_ref is not None:
                        value += add_ref[t].astype(F32)
                    value = value.astype(BF)
                    if blocks == 1:
                        outs[0][t] = value
                    else:
                        for b in range(blocks):
                            outs[b * parts + t][...] = value[b * low : (b + 1) * low]

    in_specs, operands = [], []
    for i, (left, right) in enumerate(pairs):
        in_specs.append(pl.BlockSpec((rows, height), lambda j: (0, section)))
        operands.append(left)
        per = right.shape[2] // parts // bn
        for t in range(parts):

            def where(j, i=i, t=t, per=per):
                local = jnp.clip(j - starts[i], 0, counts[i] - 1)
                return local // per, 0, t * per + local % per

            in_specs.append(pl.BlockSpec((None, rows, bn), where))
            operands.append(right)
    if add is not None:
        in_specs.append(pl.BlockSpec((parts, height, bn), lambda j: (0, 0, j)))
        operands.append(add)
    if blocks == 1:
        out_specs = pl.BlockSpec((parts, height, bn), lambda j: (0, 0, j))
        out_shape = jax.ShapeDtypeStruct((parts, height, columns), BF)
    else:
        out_specs = [pl.BlockSpec((low, bn), lambda j: (0, j))] * (blocks * parts)
        out_shape = [jax.ShapeDtypeStruct((low, columns), BF)] * (blocks * parts)
    found = pl.pallas_call(
        kernel,
        grid=(sum(counts),),
        in_specs=in_specs,
        out_specs=out_specs,
        out_shape=out_shape,
        scratch_shapes=[pltpu.VMEM((height, rows), BF) for _ in pairs],
        cost_estimate=cost(name, 2 * height * rows * columns * parts, *[p[1] for p in pairs]),
        name=name,
    )(*operands)
    if blocks == 1:
        return found
    return [[found[b * parts + t] for t in range(parts)] for b in range(blocks)]


def three_parts(value):
    first = lax.reduce_precision(value, 8, 7)
    second = lax.reduce_precision(value - first, 8, 7)
    return [part.astype(BF) for part in (first, second, value - first - second)]


def pack_small(row, height):
    flat = jnp.concatenate(three_parts(row))
    columns = -(-flat.shape[0] // (128 * height)) * 128
    return jnp.pad(flat, (0, height * columns - flat.shape[0])).reshape(height, columns)


def unpack_small(packed, size, height):
    depth = lax.axis_size("dp")
    flat = packed.reshape(-1, depth, height * packed.shape[1])[:, :, : 3 * size]
    parts = jnp.sum(flat.reshape(-1, depth, 3, size).astype(F32), axis=2)
    return jnp.swapaxes(parts, 0, 1).reshape(-1, size)


def swap(value, mask):
    count = lax.axis_size("dp") * lax.axis_size("thi") * lax.axis_size("tlo")
    return lax.ppermute(value, RANKS, [(i, i ^ mask) for i in range(count)])


def relative_small(parts):
    return jnp.take(parts, jnp.arange(parts.shape[0]) ^ lax.axis_index(RANKS), axis=0)


def scatter_small(held, until):
    mask = held.shape[0] // 2
    while mask >= until:
        held = held[:mask] + swap(held[mask:], mask)
        mask //= 2
    return held


def over_dp(value, mask):
    count = lax.axis_size("dp")
    return lax.ppermute(value, "dp", [(i, i ^ mask) for i in range(count)])


def over_tensor(value, mask):
    count = lax.axis_size("thi") * lax.axis_size("tlo")
    return lax.ppermute(value, ("thi", "tlo"), [(i, i ^ mask) for i in range(count)])


def tensor_size():
    return lax.axis_size("thi") * lax.axis_size("tlo")


def hold(*trees):
    return lax.optimization_barrier(trees)


def after(tree, *others):
    return lax.optimization_barrier((tree, others))[0]


def gather_far(shard):
    rest = lax.axis_size("dp") // 4
    return jnp.concatenate([shard] + [over_dp(shard, 4 * m) for m in range(1, rest)], axis=0)


def gather_sides(own):
    return over_dp(own, 2), [over_tensor(own, m) for m in range(1, tensor_size())]


def gather_corners(own, sides):
    across, near = sides
    half = own.shape[0] // 2
    far = [
        jnp.concatenate([over_dp(block[:half], 2), over_tensor(across[half:], m + 1)], axis=0)
        for m, block in enumerate(near)
    ]
    return [[own] + near, [across] + far]


def gather_core(here):
    return [here, [[over_dp(block, 1) for block in line] for line in here]]


def block_views(blocks, first):
    return [
        [(line[t], None, line[t].shape[0], first) for half in blocks for line in half]
        for t in range(len(blocks[0][0]))
    ]


def wide(value):
    return value.astype(F32)


def scatter_corners(line):
    half = line[0][0].shape[0] // 2
    return (
        [over_dp(block[:half], 2) for block in line[1][1:]],
        [over_tensor(block[half:], m + 1) for m, block in enumerate(line[1][1:])],
    )


def scatter_sum(line, corners):
    near, across = line[0][1:], line[1][0]
    half = across.shape[0] // 2
    tops, bottoms = corners
    near = [
        jnp.concatenate([(wide(a[:half]) + wide(b)).astype(BF), a[half:]], axis=0)
        for a, b in zip(near, tops)
    ]
    if bottoms:
        low = (wide(across[half:]) + sum(wide(b) for b in bottoms)).astype(BF)
        across = jnp.concatenate([across[:half], low], axis=0)
    return [across] + near


def scatter_sides(sums):
    return [over_dp(sums[0], 2)] + [over_tensor(v, m + 1) for m, v in enumerate(sums[1:])]


def scatter_pieces(line, sides):
    own = line[0][0]
    rest = lax.axis_size("dp") // 4
    height = own.shape[0] // rest
    piece = lambda m: sum(
        (wide(v[m * height : (m + 1) * height]) for v in sides),
        wide(own[m * height : (m + 1) * height]),
    )
    return [piece(0)] + [piece(m).astype(BF) for m in range(1, rest)]


def scatter_far(pieces):
    return [pieces[0]] + [over_dp(piece, 4 * m) for m, piece in enumerate(pieces) if m]


def scatter_end(addends):
    return sum(wide(v) for v in addends)


def relative_blocks():
    depth = lax.axis_size("dp")
    rest = depth // 4
    own = lax.axis_index("dp")
    place = np.arange(depth)
    core, second, far = place // (2 * rest), place // rest % 2, place % rest
    order = jnp.asarray(far * 4 + second * 2 + core) ^ own
    mask = jnp.arange(depth) ^ own
    places = ((mask & 1) * 2 + (mask >> 1 & 1)) * rest + (mask >> 2)
    return order, places


def reorder(rows, order):
    cut = rows.reshape(rows.shape[:-1] + (order.shape[0], -1))
    return jnp.take(cut, order, axis=-2).reshape(rows.shape)


def selection(order, width):
    each = width // order.shape[0]
    source = (order[:, None] * each + jnp.arange(each)[None]).reshape(-1)
    return (jnp.arange(width)[:, None] == source[None, :]).astype(BF)


def select_wide(rows, chooser):
    return sum(dot(part, chooser) for part in three_parts(rows))


def on_device(
    inputs,
    seg_ids,
    qkv_weight,
    out_weight,
    up_weight,
    down_weight,
    norm_gains,
    row_biases,
    ff_bias,
    cotangent,
):
    blocks = tensor_size()
    sharers = lax.axis_size("tlo")
    rows, width = inputs.shape
    layers = qkv_weight.shape[0]
    head_cols = qkv_weight.shape[3]
    hidden = up_weight.shape[2]
    length = seg_ids.shape[1]
    sets = max(1, rows // length)
    T = range(blocks)

    seg_k = lax.dynamic_slice_in_dim(seg_ids, lax.axis_index("thi") * sets, sets)
    seg_q = seg_k
    if sharers > 1:
        seg_q = lax.dynamic_slice_in_dim(seg_k, lax.axis_index("tlo") * rows, rows, axis=1)

    order, places = relative_blocks()
    pick, unpick = selection(order, width), selection(places, width)
    own_t = lax.axis_index(("thi", "tlo"))
    relative_t = (jnp.arange(blocks, dtype=jnp.int32) ^ own_t).astype(jnp.int32)

    join = lambda *parts: jnp.concatenate(parts, axis=1).astype(BF)
    qkv_of = lambda l: [qkv_weight[l, k] for k in range(3)]
    spread = lambda shard: lax.all_gather(shard, SPREAD, axis=0, tiled=True)
    views = lambda whole, first: [[(whole, t, width, first)] for t in T]
    row = jnp.concatenate([norm_gains.reshape(-1), row_biases.reshape(-1), ff_bias.reshape(-1)])
    height = qkv_weight.shape[2]
    first_whole = spread(jnp.concatenate([join(*qkv_of(0)), pack_small(row, height)], axis=1))
    small = unpack_small(first_whole[:, 3 * head_cols :], row.shape[0], height)
    later_views = [None]
    for l in range(1, layers):
        whole = spread(join(*qkv_of(l), out_weight[l].T, up_weight[l], down_weight[l].T))
        firsts = (0, 3 * head_cols, 4 * head_cols, 4 * head_cols + hidden)
        later_views.append([views(whole, first) for first in firsts])
    mid_own = gather_far(join(up_weight[0], out_weight[0].T))
    down_shard = join(down_weight[0].T)
    mid_own, down_shard = hold(mid_own, down_shard)
    mid_sides = gather_sides(mid_own)
    down_own = gather_far(down_shard)
    mid_here = gather_corners(mid_own, mid_sides)
    mid_blocks = gather_core(mid_here)
    down_own, mid_here = hold(down_own, mid_here)
    down_sides = gather_sides(down_own)

    devices = small.shape[0]
    cuts = np.cumsum([norm_gains.size, row_biases.size])
    spread_out = lambda piece, like: jnp.moveaxis(
        piece.reshape((devices,) + like.shape), 0, -2
    ).reshape(like.shape[:-1] + (devices * like.shape[-1],))
    gain_rows = spread_out(small[:, : cuts[0]], norm_gains)
    shift_rows = spread_out(small[:, cuts[0] : cuts[1]], row_biases)
    up_shifts = spread_out(small[:, cuts[1] :], ff_bias)

    def vectors(l):
        gains, shifts, up_shift = gain_rows[l], shift_rows[l], up_shifts[l]
        heads, wide = reorder(shifts[:2], relative_t), shifts[2:]
        up_shift = reorder(up_shift, relative_t)
        if l == 0:
            gains, wide = reorder(gains, order), reorder(wide, order)
        heads = heads.reshape(2, blocks, head_cols)
        qkv_shift = jnp.stack([heads[0], jnp.zeros_like(heads[0]), heads[1]], axis=1)
        return gains, qkv_shift.reshape(1, -1), wide, up_shift[None]

    add_shift = lambda value, shift: (value + shift,)

    def enter(value, shift):
        value = value + shift
        upto = 0.5 * (1.0 + lax.erf(value * HALF_ROOT))
        return value * upto, upto + value * jnp.exp(-0.5 * value * value) * INV_ROOT_TAU

    def leave(value, slope):
        return (value * slope.astype(F32),)

    gather_keys = (
        (lambda v: lax.all_gather(v, "tlo", axis=0, tiled=True)) if sharers > 1 else (lambda v: v)
    )
    stored = []
    stream = dot(inputs, pick)
    for l in range(layers):
        gains, qkv_shift, shifts, up_shift = vectors(l)
        if l == 1:
            stream = select_wide(stream, unpick)
        if l == 0:
            qkv, low = views(first_whole, 0), inputs
        else:
            qkv, out, up, down = later_views[l]
            low = stream.astype(BF)
        (projected,) = times_weight(
            relative_t, low, qkv, 3 * head_cols, add_shift, [qkv_shift], [BF], "project"
        )
        if l == 0:
            projected, down_sides = hold(projected, down_sides)
            down_here = gather_corners(down_own, down_sides)
        keys = gather_keys(projected)
        mixture = attend(projected, keys, head_cols, seg_q, seg_k)
        if l == 0:
            mixture, down_here = hold(mixture, down_here)
            up, out = block_views(mid_blocks, 0), block_views(mid_blocks, hidden)
            down = block_views(gather_core(down_here), 0)
        attended = times_transposed(relative_t, mixture[None], out, "attended")
        unit_early, rate_early = norm_parts(stream + (attended + shifts[0]))
        mid = unit_early * gains[0] + shifts[1]
        mid_low = mid.astype(BF)
        hidden_out, slopes = times_weight(
            relative_t, mid_low, up, hidden, enter, [up_shift], [BF, BF], "enter"
        )
        branch = times_transposed(relative_t, hidden_out[None], down, "branch")
        unit_late, rate_late = norm_parts(mid + (branch + shifts[2]))
        stored.append(
            (
                qkv,
                out,
                up,
                down,
                gains,
                low,
                projected,
                keys,
                mixture,
                unit_early,
                rate_early,
                mid_low,
                slopes,
                hidden_out,
                unit_late,
                rate_late,
            )
        )
        stream = unit_late * gains[1] + shifts[3]
    if layers == 1:
        stream = select_wide(stream, unpick)

    grad_stream = cotangent
    mlp_done, attn_done = [None] * layers, [None] * layers
    small_grads = [None] * layers
    over_rows = lambda value: jnp.sum(value.astype(F32), axis=0)
    fold = lambda whole: jnp.moveaxis(
        whole.reshape(whole.shape[:-1] + (devices, whole.shape[-1] // devices)), -2, 0
    ).reshape(devices, -1)
    flying = None
    for l in reversed(range(layers)):
        (
            qkv,
            out,
            up,
            down,
            gains,
            low,
            projected,
            keys,
            mixture,
            unit_early,
            rate_early,
            mid_low,
            slopes,
            hidden_out,
            unit_late,
            rate_late,
        ) = stored[l]
        if l == 0:
            grad_stream = select_wide(grad_stream, pick)
        grad_second = norm_back(grad_stream, unit_late, rate_late, gains[1])
        gain_late, shift_late = over_rows(grad_stream * unit_late), over_rows(grad_stream)
        second_low = grad_second.astype(BF)
        (grad_pre,) = times_weight(relative_t, second_low, down, hidden, leave, [slopes], [BF], "leave")
        if flying is not None:
            line, corners, other_line, other_sides = flying
            grad_pre, corners, other_sides = hold(grad_pre, corners, other_sides)
            sums = scatter_sum(line, corners)
            pieces = scatter_pieces(other_line, other_sides)
            grad_pre, sums, pieces = hold(grad_pre, sums, pieces)
            sides, other_addends = scatter_sides(sums), scatter_far(pieces)
        turned = (lambda v: v) if l == 0 else (lambda v: dot(v, pick).astype(BF))
        mlp_pairs = [(turned(mid_low), grad_pre[None]), (turned(second_low), hidden_out[None])]
        mlp_send = weight_grads(mlp_pairs, blocks, 1, 2, name="mlp_send")
        mlp_send, grad_pre = hold(mlp_send, grad_pre)
        mlp_came = over_dp(mlp_send, 1)
        back = times_transposed(relative_t, grad_pre[None], up, "grad_mid")
        mlp_line = weight_grads(
            mlp_pairs, blocks, 0, 2, add=after(mlp_came, back), blocks=2, name="mlp_keep"
        )
        mlp_line, back = hold(mlp_line, back)
        mlp_corners = scatter_corners(mlp_line)
        grad_mid = grad_second + back
        grad_first = norm_back(grad_mid, unit_early, rate_early, gains[0])
        gain_early, shift_early = over_rows(grad_mid * unit_early), over_rows(grad_mid)
        first_low = grad_first.astype(BF)
        if flying is not None:
            first_low, sides, other_addends = hold(first_low, sides, other_addends)
            pieces = scatter_pieces(line, sides)
            mlp_done[l + 1] = scatter_end(other_addends)
            first_low, pieces = hold(first_low, pieces)
            addends = scatter_far(pieces)
        (grad_mix,) = times_weight(
            relative_t, first_low, out, head_cols, lambda v: (v,), [], [BF], "grad_mix"
        )
        grad_mix, mlp_corners = hold(grad_mix, mlp_corners)
        mlp_sums = scatter_sum(mlp_line, mlp_corners)
        grad_mix, mlp_sums = hold(grad_mix, mlp_sums)
        mlp_sides = scatter_sides(mlp_sums)
        grad_proj = attend_back(projected, keys, head_cols, grad_mix, seg_q, seg_k)
        if sharers > 1:
            grad_proj = jnp.stack(
                [grad_proj[0]]
                + [
                    lax.psum_scatter(v, "tlo", scatter_dimension=0, tiled=True).astype(BF)
                    for v in grad_proj[1:]
                ]
            )
        left = dot(low, pick).astype(BF)
        attn_pairs = [(left, grad_proj), (turned(first_low), mixture[None])]
        attn_send = weight_grads(attn_pairs, blocks, 1, 2, name="attn_send")
        if flying is not None:
            attn_send, addends = hold(attn_send, addends)
            attn_done[l + 1] = scatter_end(addends)
        if l == 0:
            attn_send, grad_proj, mlp_sides = hold(attn_send, grad_proj, mlp_sides)
            mlp_pieces = scatter_pieces(mlp_line, mlp_sides)
            attn_send, grad_proj, mlp_pieces = hold(attn_send, grad_proj, mlp_pieces)
            mlp_addends = scatter_far(mlp_pieces)
        else:
            attn_send, grad_proj = hold(attn_send, grad_proj)
        attn_came = over_dp(attn_send, 1)
        back = times_transposed(relative_t, grad_proj, qkv, "grad_stream")
        back, attn_came = hold(back, attn_came)
        attn_line = weight_grads(
            attn_pairs, blocks, 0, 2, add=attn_came, blocks=2, name="attn_keep"
        )
        wide_grad = jnp.stack(
            [over_rows(grad_first), shift_early, over_rows(grad_second), shift_late]
        )
        gains_grad = jnp.stack([gain_early, gain_late])
        if l == 0:
            wide_grad, gains_grad = reorder(wide_grad, places), reorder(gains_grad, places)
        small_grads[l] = gains_grad, wide_grad, grad_proj, grad_pre
        if l == 0:
            attn_line, back = hold(attn_line, back)
            attn_corners = scatter_corners(attn_line)
            held = after(small_grads, attn_line)
            heads_grads = [jnp.stack([over_rows(h[2][0]), over_rows(h[2][2])]) for h in held]
            smalls = (
                jnp.stack([h[0] for h in held]),
                jnp.concatenate(
                    [
                        reorder(jnp.stack(heads_grads), relative_t),
                        jnp.stack([h[1] for h in held]),
                    ],
                    axis=1,
                ),
                reorder(jnp.stack([over_rows(h[3]) for h in held]), relative_t),
            )
            small_sums = relative_small(
                jnp.concatenate([fold(whole) for whole in smalls], axis=1)
            )
            attn_sums = scatter_sum(*after((attn_line, attn_corners), small_sums))
            attn_sides = scatter_sides(attn_sums)
            mlp_addends, small_sums = after((mlp_addends, small_sums), attn_sums)
            mlp_done[l] = scatter_end(mlp_addends)
            small_sums = scatter_small(after(small_sums, mlp_done[l]), 4 * blocks)
            attn_sides, small_sums = hold(attn_sides, small_sums)
            attn_pieces = scatter_pieces(attn_line, attn_sides)
            attn_pieces, small_sums = hold(attn_pieces, small_sums)
            attn_addends = scatter_far(attn_pieces)
            summed = scatter_small(small_sums, 1)[0]
            attn_done[l] = scatter_end(after(attn_addends, summed))
            input_grad = select_wide(after(grad_first, attn_line), unpick) + back
        else:
            attn_line, back = hold(attn_line, back)
            flying = attn_line, scatter_corners(attn_line), mlp_line, mlp_sides
            grad_stream = grad_first + back

    return (
        stream.astype(BF),
        input_grad,
        jnp.stack(
            [
                jnp.stack(
                    [attn_done[l][:, k * head_cols : (k + 1) * head_cols] for k in range(3)]
                )
                for l in range(layers)
            ]
        ),
        jnp.stack([attn_done[l][:, 3 * head_cols :].T for l in range(layers)]),
        jnp.stack([mlp_done[l][:, :hidden] for l in range(layers)]),
        jnp.stack([mlp_done[l][:, hidden:].T for l in range(layers)]),
        summed[: cuts[0]].reshape(norm_gains.shape),
        summed[cuts[0] : cuts[1]].reshape(row_biases.shape),
        summed[cuts[1] :].reshape(ff_bias.shape),
    )


def solution(mesh):
    def whole(*args):
        inputs, seg_ids = args[:2]
        depth, blocks = mesh.shape["dp"], mesh.shape["tensor"]
        rows = inputs.shape[0] // (depth * blocks)
        sharers = max(1, seg_ids.shape[1] // rows)
        inner = Mesh(mesh.devices.reshape(depth, blocks // sharers, sharers), RANKS)
        tensor = ("thi", "tlo")
        row_wise = P(RANKS, None)
        weight_specs = (
            P(None, None, "dp", tensor),
            P(None, tensor, "dp"),
            P(None, "dp", tensor),
            P(None, tensor, "dp"),
            P(None, None, RANKS),
            P(None, None, RANKS),
            P(None, RANKS),
        )
        return jax.shard_map(
            on_device,
            mesh=inner,
            in_specs=(row_wise, P("dp", None)) + weight_specs + (row_wise,),
            out_specs=(row_wise, row_wise) + weight_specs,
            check_vma=False,
        )(*args)

    return whole
```

```python
from functools import partial

import jax
import jax.numpy as jnp
import numpy as np
from jax import lax
from jax.experimental import pallas as pl
from jax.experimental.pallas import tpu as pltpu
from jax.sharding import Mesh
from jax.sharding import PartitionSpec as P

HD = 64
EPSILON = 1e-06
HALF_ROOT = 0.7071067811865476
INV_ROOT_TAU = 0.3989422804014327
BF = jnp.bfloat16
F32 = jnp.float32
RANKS = ("dp", "thi", "tlo")
SPREAD = ("thi", "tlo", "dp")


def norm_parts(summed):
    centre = summed - jnp.mean(summed, axis=-1, keepdims=True)
    spread = jnp.mean(centre * centre, axis=-1, keepdims=True)
    rate = lax.rsqrt(spread + EPSILON)
    return centre * rate, rate


def norm_back(grad, unit, rate, gain):
    scaled = grad * gain
    return rate * (
        scaled
        - jnp.mean(scaled, axis=-1, keepdims=True)
        - unit * jnp.mean(scaled * unit, axis=-1, keepdims=True)
    )


def dot(a, b):
    return jnp.dot(a, b, preferred_element_type=F32)


def dot_nt(a, b):
    return lax.dot_general(a, b, (((1,), (1,)), ((), ())), preferred_element_type=F32)


def dot_tn(a, b):
    return lax.dot_general(a, b, (((0,), (0,)), ((), ())), preferred_element_type=F32)


def attend_kernel(q_ref, k_ref, v_ref, segq_ref, segk_ref, out_ref):
    same = segk_ref[0] == segq_ref[0]
    outs = []
    for half in range(q_ref.shape[1] // HD):
        cols = slice(half * HD, half * HD + HD)
        q = (q_ref[:, cols].astype(F32) * HD ** (-0.5)).astype(BF)
        scores = jnp.where(same, dot_nt(k_ref[:, cols], q), -jnp.inf)
        top = jnp.max(scores, axis=0, keepdims=True)
        weights = jnp.exp(scores - top)
        total = jnp.sum(weights, axis=0, keepdims=True)
        probs = (weights * (1.0 / total)).astype(BF)
        outs.append(dot_tn(probs, v_ref[:, cols]))
    out_ref[...] = jnp.concatenate(outs, axis=1).astype(BF)


def attend_back_kernel(q_ref, k_ref, v_ref, grad_ref, segq_ref, segk_ref, *out_refs):
    same = segk_ref[0] == segq_ref[0]
    found = [], [], []
    for half in range(q_ref.shape[1] // HD):
        cols = slice(half * HD, half * HD + HD)
        q = (q_ref[:, cols].astype(F32) * HD ** (-0.5)).astype(BF)
        k, v, grad = k_ref[:, cols], v_ref[:, cols], grad_ref[:, cols]
        scores = jnp.where(same, dot_nt(k, q), -jnp.inf)
        top = jnp.max(scores, axis=0, keepdims=True)
        weights = jnp.exp(scores - top)
        probs = weights * (1.0 / jnp.sum(weights, axis=0, keepdims=True))
        grad_probs = dot_nt(v, grad)
        inner = jnp.sum(grad_probs * probs, axis=0, keepdims=True)
        grad_scores = (probs * (grad_probs - inner)).astype(BF)
        found[0].append(dot_tn(grad_scores, k) * HD ** (-0.5))
        found[1].append(dot(grad_scores, q))
        found[2].append(dot(probs.astype(BF), grad))
    for i in range(3):
        target = out_refs[0].at[i] if len(out_refs) == 1 else out_refs[i]
        target[...] = jnp.concatenate(found[i], axis=1).astype(target.dtype)


def attention_specs(rows, keys, cols):
    wide = 128 if cols % 128 == 0 else cols
    pairs = cols // wide
    part = lambda n, k: pl.BlockSpec(
        (n, wide), lambda s, j: (s, (j // pairs * 3 + k) * pairs + j % pairs)
    )
    plain = lambda n: pl.BlockSpec((n, wide), lambda s, j: (s, j))
    segs = [
        pl.BlockSpec((1, 1, rows), lambda s, j: (s, 0, 0)),
        pl.BlockSpec((1, keys, 1), lambda s, j: (s, 0, 0)),
    ]
    return wide, pairs, [part(rows, 0), part(keys, 1), part(keys, 2)], plain, segs


def attend(q, kv, cols, seg_q, seg_k):
    sets, parts = seg_q.shape[0], q.shape[1] // (3 * cols)
    rows, keys = q.shape[0] // sets, kv.shape[0] // sets
    _, pairs, specs, plain, segs = attention_specs(rows, keys, cols)
    work = parts * cols // HD * sets * rows * keys
    return pl.pallas_call(
        attend_kernel,
        grid=(sets, parts * pairs),
        in_specs=specs + segs,
        out_specs=plain(rows),
        out_shape=jax.ShapeDtypeStruct((q.shape[0], parts * cols), BF),
        cost_estimate=pl.CostEstimate(
            flops=16 * work * HD, bytes_accessed=2 * q.size * 2, transcendentals=work
        ),
        name="attend",
    )(q, kv, kv, seg_q[:, None, :], seg_k[:, :, None])


def attend_back(q, kv, cols, grad, seg_q, seg_k):
    sets, parts = seg_q.shape[0], q.shape[1] // (3 * cols)
    rows, keys = q.shape[0] // sets, kv.shape[0] // sets
    wide, pairs, specs, plain, segs = attention_specs(rows, keys, cols)
    work = parts * cols // HD * sets * rows * keys
    if rows == keys:
        out_specs = pl.BlockSpec((3, rows, wide), lambda s, j: (0, s, j))
        out_shape = jax.ShapeDtypeStruct((3, q.shape[0], parts * cols), BF)
    else:
        out_specs = [plain(rows), plain(keys), plain(keys)]
        out_shape = [
            jax.ShapeDtypeStruct((q.shape[0], parts * cols), BF),
            jax.ShapeDtypeStruct((kv.shape[0], parts * cols), F32),
            jax.ShapeDtypeStruct((kv.shape[0], parts * cols), F32),
        ]
    return pl.pallas_call(
        attend_back_kernel,
        grid=(sets, parts * pairs),
        in_specs=specs + [plain(rows)] + segs,
        out_specs=out_specs,
        out_shape=out_shape,
        cost_estimate=pl.CostEstimate(
            flops=5 * work * HD, bytes_accessed=q.size, transcendentals=work // 8
        ),
        name="attend_back",
    )(q, kv, kv, grad, seg_q[:, None, :], seg_k[:, :, None])


def tile(most, *sizes):
    for size in (1024, 768, 512, 384, 256, 128):
        if size <= most and all(n % size == 0 for n in sizes):
            return size
    raise ValueError("width")


def cost(name, flops, *arrays):
    short = 1 if name in ("project", "attended", "enter", "branch") else 8
    return pl.CostEstimate(
        flops=flops // short,
        bytes_accessed=sum(a.size * a.dtype.itemsize for a in arrays) // short,
        transcendentals=0,
    )


def times_weight(which, x, weight, cols, finish, extras, out_types, name):
    rows, parts, count = x.shape[0], len(weight), len(weight[0])
    bn = tile(1024, cols, *[v[3] for w in weight for v in w])
    per = cols // bn

    def spec(t, view):
        _, block, height, first = view
        local = lambda j: first // bn + jnp.clip(j - t * per, 0, per - 1)
        if block is None:
            return pl.BlockSpec((height, bn), lambda j, _: (0, local(j)))
        return pl.BlockSpec((height, bn), lambda j, names: (names[block], local(j)))

    def kernel(which_ref, x_ref, *refs):
        step = pl.program_id(0)
        more = refs[parts * count : parts * count + len(extras)]
        outs = refs[parts * count + len(extras) :]
        for t in range(parts):

            @pl.when((step >= t * per) & (step < t * per + per))
            def _(t=t):
                total, first = None, 0
                for ref in refs[t * count : (t + 1) * count]:
                    height = ref.shape[0]
                    part = dot(x_ref[:, first : first + height], ref[...])
                    total = part if total is None else total + part
                    first += height
                for ref, out in zip(outs, finish(total, *[e[...] for e in more])):
                    ref[...] = out.astype(ref.dtype)

    return pl.pallas_call(
        kernel,
        grid_spec=pltpu.PrefetchScalarGridSpec(
            num_scalar_prefetch=1,
            grid=(parts * per,),
            in_specs=[pl.BlockSpec(x.shape, lambda j, _: (0, 0))]
            + [spec(t, v) for t in range(parts) for v in weight[t]]
            + [pl.BlockSpec((e.shape[0], bn), lambda j, _: (0, j)) for e in extras],
            out_specs=[pl.BlockSpec((rows, bn), lambda j, _: (0, j)) for _ in out_types],
        ),
        out_shape=[jax.ShapeDtypeStruct((rows, parts * cols), t) for t in out_types],
        cost_estimate=cost(name, 2 * x.size * cols * parts, x, x),
        name=name,
    )(which, x, *[v[0] for w in weight for v in w], *extras)


def times_transposed(which, right, weight, name):
    parts = len(weight)
    stack, rows, each = right.shape[0], right.shape[1], right.shape[2] // parts
    bn = tile(1024, each, *[v[3] for w in weight for v in w])
    per = each // bn
    heights = [v[2] for v in weight[0]]
    width = sum(heights)

    def spec(view):
        _, block, height, first = view
        if block is None:
            return pl.BlockSpec((height, bn), lambda j, _: (0, first // bn + j))
        return pl.BlockSpec((height, bn), lambda j, names: (names[block], first // bn + j))

    def kernel(which_ref, *refs):
        out_ref = refs[-1]
        begin = pl.program_id(0) == 0
        place = 0
        for b, height in enumerate(heights):
            cols = slice(place, place + height)
            total = sum(
                dot_nt(refs[t][...], refs[parts + t * len(heights) + b][...])
                for t in range(parts)
            )
            if stack * per == 1:
                out_ref[:, cols] = total
            else:

                @pl.when(begin)
                def _():
                    out_ref[:, cols] = total

                @pl.when(jnp.logical_not(begin))
                def _():
                    out_ref[:, cols] += total

            place += height

    return pl.pallas_call(
        kernel,
        grid_spec=pltpu.PrefetchScalarGridSpec(
            num_scalar_prefetch=1,
            grid=(stack * per,),
            in_specs=[
                pl.BlockSpec(
                    (None, rows, bn), lambda j, _, t=t: (j // per, 0, t * per + j % per)
                )
                for t in range(parts)
            ]
            + [spec(v) for w in weight for v in w],
            out_specs=pl.BlockSpec((rows, width), lambda j, _: (0, 0)),
        ),
        out_shape=jax.ShapeDtypeStruct((rows, width), F32),
        cost_estimate=cost(name, 2 * rows * width * stack * each * parts, right),
        name=name,
    )(which, *[right] * parts, *[v[0] for w in weight for v in w])


def weight_grads(pairs, parts, section, sections, add=None, blocks=1, name="weight_grads"):
    rows, width = pairs[0][0].shape
    height = width // sections
    bn = tile(1024, *[right.shape[2] // parts for _, right in pairs])
    counts = [right.shape[0] * right.shape[2] // parts // bn for _, right in pairs]
    starts = [sum(counts[:i]) for i in range(len(pairs))]
    columns = sum(counts) * bn
    low = height // blocks

    def kernel(*refs):
        step = pl.program_id(0)
        turned = refs[-len(pairs) :]
        at = len(pairs) * (1 + parts)
        add_ref = refs[at] if add is not None else None
        outs = refs[at + (add is not None) : -len(pairs)]
        for i in range(len(pairs)):
            base = i * (1 + parts)

            @pl.when(step == starts[i])
            def _(i=i, base=base):
                turned[i][...] = refs[base][...].T

            @pl.when((step >= starts[i]) & (step < starts[i] + counts[i]))
            def _(i=i, base=base):
                for t in range(parts):
                    value = dot(turned[i][...], refs[base + 1 + t][...])
                    if add_ref is not None:
                        value += add_ref[t].astype(F32)
                    value = value.astype(BF)
                    if blocks == 1:
                        outs[0][t] = value
                    else:
                        for b in range(blocks):
                            outs[b * parts + t][...] = value[b * low : (b + 1) * low]

    in_specs, operands = [], []
    for i, (left, right) in enumerate(pairs):
        in_specs.append(pl.BlockSpec((rows, height), lambda j: (0, section)))
        operands.append(left)
        per = right.shape[2] // parts // bn
        for t in range(parts):

            def where(j, i=i, t=t, per=per):
                local = jnp.clip(j - starts[i], 0, counts[i] - 1)
                return local // per, 0, t * per + local % per

            in_specs.append(pl.BlockSpec((None, rows, bn), where))
            operands.append(right)
    if add is not None:
        in_specs.append(pl.BlockSpec((parts, height, bn), lambda j: (0, 0, j)))
        operands.append(add)
    if blocks == 1:
        out_specs = pl.BlockSpec((parts, height, bn), lambda j: (0, 0, j))
        out_shape = jax.ShapeDtypeStruct((parts, height, columns), BF)
    else:
        out_specs = [pl.BlockSpec((low, bn), lambda j: (0, j))] * (blocks * parts)
        out_shape = [jax.ShapeDtypeStruct((low, columns), BF)] * (blocks * parts)
    found = pl.pallas_call(
        kernel,
        grid=(sum(counts),),
        in_specs=in_specs,
        out_specs=out_specs,
        out_shape=out_shape,
        scratch_shapes=[pltpu.VMEM((height, rows), BF) for _ in pairs],
        cost_estimate=cost(name, 2 * height * rows * columns * parts, *[p[1] for p in pairs]),
        name=name,
    )(*operands)
    if blocks == 1:
        return found
    return [[found[b * parts + t] for t in range(parts)] for b in range(blocks)]


def three_parts(value):
    first = lax.reduce_precision(value, 8, 7)
    second = lax.reduce_precision(value - first, 8, 7)
    return [part.astype(BF) for part in (first, second, value - first - second)]


def pack_small(row, height):
    flat = jnp.concatenate(three_parts(row))
    columns = -(-flat.shape[0] // (128 * height)) * 128
    return jnp.pad(flat, (0, height * columns - flat.shape[0])).reshape(height, columns)


def unpack_small(packed, size, height):
    depth = lax.axis_size("dp")
    flat = packed.reshape(-1, depth, height * packed.shape[1])[:, :, : 3 * size]
    parts = jnp.sum(flat.reshape(-1, depth, 3, size).astype(F32), axis=2)
    return jnp.swapaxes(parts, 0, 1).reshape(-1, size)


def swap(value, mask):
    count = lax.axis_size("dp") * lax.axis_size("thi") * lax.axis_size("tlo")
    return lax.ppermute(value, RANKS, [(i, i ^ mask) for i in range(count)])


def relative_small(parts):
    return jnp.take(parts, jnp.arange(parts.shape[0]) ^ lax.axis_index(RANKS), axis=0)


def scatter_small(held, until):
    mask = held.shape[0] // 2
    while mask >= until:
        held = held[:mask] + swap(held[mask:], mask)
        mask //= 2
    return held


def over_dp(value, mask):
    count = lax.axis_size("dp")
    return lax.ppermute(value, "dp", [(i, i ^ mask) for i in range(count)])


def over_tensor(value, mask):
    count = lax.axis_size("thi") * lax.axis_size("tlo")
    return lax.ppermute(value, ("thi", "tlo"), [(i, i ^ mask) for i in range(count)])


def tensor_size():
    return lax.axis_size("thi") * lax.axis_size("tlo")


def hold(*trees):
    return lax.optimization_barrier(trees)


def after(tree, *others):
    return lax.optimization_barrier((tree, others))[0]


def gather_far(shard):
    rest = lax.axis_size("dp") // 4
    return jnp.concatenate([shard] + [over_dp(shard, 4 * m) for m in range(1, rest)], axis=0)


def gather_sides(own):
    return over_dp(own, 2), [over_tensor(own, m) for m in range(1, tensor_size())]


def gather_corners(own, sides):
    across, near = sides
    half = own.shape[0] // 2
    far = [
        jnp.concatenate([over_dp(block[:half], 2), over_tensor(across[half:], m + 1)], axis=0)
        for m, block in enumerate(near)
    ]
    return [[own] + near, [across] + far]


def gather_core(here):
    return [here, [[over_dp(block, 1) for block in line] for line in here]]


def block_views(blocks, first):
    return [
        [(line[t], None, line[t].shape[0], first) for half in blocks for line in half]
        for t in range(len(blocks[0][0]))
    ]


def wide(value):
    return value.astype(F32)


def scatter_corners(line):
    half = line[0][0].shape[0] // 2
    return (
        [over_dp(block[:half], 2) for block in line[1][1:]],
        [over_tensor(block[half:], m + 1) for m, block in enumerate(line[1][1:])],
    )


def scatter_sum(line, corners):
    near, across = line[0][1:], line[1][0]
    half = across.shape[0] // 2
    tops, bottoms = corners
    near = [
        jnp.concatenate([(wide(a[:half]) + wide(b)).astype(BF), a[half:]], axis=0)
        for a, b in zip(near, tops)
    ]
    if bottoms:
        low = (wide(across[half:]) + sum(wide(b) for b in bottoms)).astype(BF)
        across = jnp.concatenate([across[:half], low], axis=0)
    return [across] + near


def scatter_sides(sums):
    return [over_dp(sums[0], 2)] + [over_tensor(v, m + 1) for m, v in enumerate(sums[1:])]


def scatter_pieces(line, sides):
    own = line[0][0]
    rest = lax.axis_size("dp") // 4
    height = own.shape[0] // rest
    piece = lambda m: sum(
        (wide(v[m * height : (m + 1) * height]) for v in sides),
        wide(own[m * height : (m + 1) * height]),
    )
    return [piece(0)] + [piece(m).astype(BF) for m in range(1, rest)]


def scatter_far(pieces):
    return [pieces[0]] + [over_dp(piece, 4 * m) for m, piece in enumerate(pieces) if m]


def scatter_end(addends):
    return sum(wide(v) for v in addends)


def relative_blocks():
    depth = lax.axis_size("dp")
    rest = depth // 4
    own = lax.axis_index("dp")
    place = np.arange(depth)
    core, second, far = place // (2 * rest), place // rest % 2, place % rest
    order = jnp.asarray(far * 4 + second * 2 + core) ^ own
    mask = jnp.arange(depth) ^ own
    places = ((mask & 1) * 2 + (mask >> 1 & 1)) * rest + (mask >> 2)
    return order, places


def reorder(rows, order):
    cut = rows.reshape(rows.shape[:-1] + (order.shape[0], -1))
    return jnp.take(cut, order, axis=-2).reshape(rows.shape)


def selection(order, width):
    each = width // order.shape[0]
    source = (order[:, None] * each + jnp.arange(each)[None]).reshape(-1)
    return (jnp.arange(width)[:, None] == source[None, :]).astype(BF)


def select_wide(rows, chooser):
    return sum(dot(part, chooser) for part in three_parts(rows))


def on_device(
    inputs,
    seg_ids,
    qkv_weight,
    out_weight,
    up_weight,
    down_weight,
    norm_gains,
    row_biases,
    ff_bias,
    cotangent,
):
    blocks = tensor_size()
    sharers = lax.axis_size("tlo")
    rows, width = inputs.shape
    layers = qkv_weight.shape[0]
    head_cols = qkv_weight.shape[3]
    hidden = up_weight.shape[2]
    length = seg_ids.shape[1]
    sets = max(1, rows // length)
    T = range(blocks)

    seg_k = lax.dynamic_slice_in_dim(seg_ids, lax.axis_index("thi") * sets, sets)
    seg_q = seg_k
    if sharers > 1:
        seg_q = lax.dynamic_slice_in_dim(seg_k, lax.axis_index("tlo") * rows, rows, axis=1)

    order, places = relative_blocks()
    pick, unpick = selection(order, width), selection(places, width)
    own_t = lax.axis_index(("thi", "tlo"))
    relative_t = (jnp.arange(blocks, dtype=jnp.int32) ^ own_t).astype(jnp.int32)

    join = lambda *parts: jnp.concatenate(parts, axis=1).astype(BF)
    qkv_of = lambda l: [qkv_weight[l, k] for k in range(3)]
    spread = lambda shard: lax.all_gather(shard, SPREAD, axis=0, tiled=True)
    views = lambda whole, first: [[(whole, t, width, first)] for t in T]
    row = jnp.concatenate([norm_gains.reshape(-1), row_biases.reshape(-1), ff_bias.reshape(-1)])
    height = qkv_weight.shape[2]
    first_whole = spread(jnp.concatenate([join(*qkv_of(0)), pack_small(row, height)], axis=1))
    small = unpack_small(first_whole[:, 3 * head_cols :], row.shape[0], height)
    later_views = [None]
    for l in range(1, layers):
        whole = spread(join(*qkv_of(l), out_weight[l].T, up_weight[l], down_weight[l].T))
        firsts = (0, 3 * head_cols, 4 * head_cols, 4 * head_cols + hidden)
        later_views.append([views(whole, first) for first in firsts])
    mid_own = gather_far(join(up_weight[0], out_weight[0].T))
    down_shard = join(down_weight[0].T)
    mid_own, down_shard = hold(mid_own, down_shard)
    mid_sides = gather_sides(mid_own)
    down_own = gather_far(down_shard)
    mid_here = gather_corners(mid_own, mid_sides)
    mid_blocks = gather_core(mid_here)
    down_own, mid_here = hold(down_own, mid_here)
    down_sides = gather_sides(down_own)

    devices = small.shape[0]
    cuts = np.cumsum([norm_gains.size, row_biases.size])
    spread_out = lambda piece, like: jnp.moveaxis(
        piece.reshape((devices,) + like.shape), 0, -2
    ).reshape(like.shape[:-1] + (devices * like.shape[-1],))
    gain_rows = spread_out(small[:, : cuts[0]], norm_gains)
    shift_rows = spread_out(small[:, cuts[0] : cuts[1]], row_biases)
    up_shifts = spread_out(small[:, cuts[1] :], ff_bias)

    def vectors(l):
        gains, shifts, up_shift = gain_rows[l], shift_rows[l], up_shifts[l]
        heads, wide = reorder(shifts[:2], relative_t), shifts[2:]
        up_shift = reorder(up_shift, relative_t)
        if l == 0:
            gains, wide = reorder(gains, order), reorder(wide, order)
        heads = heads.reshape(2, blocks, head_cols)
        qkv_shift = jnp.stack([heads[0], jnp.zeros_like(heads[0]), heads[1]], axis=1)
        return gains, qkv_shift.reshape(1, -1), wide, up_shift[None]

    add_shift = lambda value, shift: (value + shift,)

    def enter(value, shift):
        value = value + shift
        upto = 0.5 * (1.0 + lax.erf(value * HALF_ROOT))
        return value * upto, upto + value * jnp.exp(-0.5 * value * value) * INV_ROOT_TAU

    def leave(value, slope):
        return (value * slope.astype(F32),)

    gather_keys = (
        (lambda v: lax.all_gather(v, "tlo", axis=0, tiled=True)) if sharers > 1 else (lambda v: v)
    )
    stored = []
    stream = dot(inputs, pick)
    for l in range(layers):
        gains, qkv_shift, shifts, up_shift = vectors(l)
        if l == 1:
            stream = select_wide(stream, unpick)
        if l == 0:
            qkv, low = views(first_whole, 0), inputs
        else:
            qkv, out, up, down = later_views[l]
            low = stream.astype(BF)
        (projected,) = times_weight(
            relative_t, low, qkv, 3 * head_cols, add_shift, [qkv_shift], [BF], "project"
        )
        if l == 0:
            projected, down_sides = hold(projected, down_sides)
            down_here = gather_corners(down_own, down_sides)
        keys = gather_keys(projected)
        mixture = attend(projected, keys, head_cols, seg_q, seg_k)
        if l == 0:
            mixture, down_here = hold(mixture, down_here)
            up, out = block_views(mid_blocks, 0), block_views(mid_blocks, hidden)
            down = block_views(gather_core(down_here), 0)
        attended = times_transposed(relative_t, mixture[None], out, "attended")
        unit_early, rate_early = norm_parts(stream + (attended + shifts[0]))
        mid = unit_early * gains[0] + shifts[1]
        mid_low = mid.astype(BF)
        hidden_out, slopes = times_weight(
            relative_t, mid_low, up, hidden, enter, [up_shift], [BF, BF], "enter"
        )
        branch = times_transposed(relative_t, hidden_out[None], down, "branch")
        unit_late, rate_late = norm_parts(mid + (branch + shifts[2]))
        stored.append(
            (
                qkv,
                out,
                up,
                down,
                gains,
                low,
                projected,
                keys,
                mixture,
                unit_early,
                rate_early,
                mid_low,
                slopes,
                hidden_out,
                unit_late,
                rate_late,
            )
        )
        stream = unit_late * gains[1] + shifts[3]
    if layers == 1:
        stream = select_wide(stream, unpick)

    grad_stream = cotangent
    mlp_done, attn_done = [None] * layers, [None] * layers
    small_grads = [None] * layers
    over_rows = lambda value: jnp.sum(value.astype(F32), axis=0)
    fold = lambda whole: jnp.moveaxis(
        whole.reshape(whole.shape[:-1] + (devices, whole.shape[-1] // devices)), -2, 0
    ).reshape(devices, -1)
    flying = None
    for l in reversed(range(layers)):
        (
            qkv,
            out,
            up,
            down,
            gains,
            low,
            projected,
            keys,
            mixture,
            unit_early,
            rate_early,
            mid_low,
            slopes,
            hidden_out,
            unit_late,
            rate_late,
        ) = stored[l]
        if l == 0:
            grad_stream = select_wide(grad_stream, pick)
        grad_second = norm_back(grad_stream, unit_late, rate_late, gains[1])
        gain_late, shift_late = over_rows(grad_stream * unit_late), over_rows(grad_stream)
        second_low = grad_second.astype(BF)
        (grad_pre,) = times_weight(relative_t, second_low, down, hidden, leave, [slopes], [BF], "leave")
        if flying is not None:
            line, corners, other_line, other_sides = flying
            grad_pre, corners, other_sides = hold(grad_pre, corners, other_sides)
            sums = scatter_sum(line, corners)
            pieces = scatter_pieces(other_line, other_sides)
            grad_pre, sums, pieces = hold(grad_pre, sums, pieces)
            sides, other_addends = scatter_sides(sums), scatter_far(pieces)
        turned = (lambda v: v) if l == 0 else (lambda v: dot(v, pick).astype(BF))
        mlp_pairs = [(turned(mid_low), grad_pre[None]), (turned(second_low), hidden_out[None])]
        mlp_send = weight_grads(mlp_pairs, blocks, 1, 2, name="mlp_send")
        mlp_send, grad_pre = hold(mlp_send, grad_pre)
        mlp_came = over_dp(mlp_send, 1)
        back = times_transposed(relative_t, grad_pre[None], up, "grad_mid")
        mlp_line = weight_grads(
            mlp_pairs, blocks, 0, 2, add=after(mlp_came, back), blocks=2, name="mlp_keep"
        )
        mlp_line, back = hold(mlp_line, back)
        mlp_corners = scatter_corners(mlp_line)
        grad_mid = grad_second + back
        grad_first = norm_back(grad_mid, unit_early, rate_early, gains[0])
        gain_early, shift_early = over_rows(grad_mid * unit_early), over_rows(grad_mid)
        first_low = grad_first.astype(BF)
        if flying is not None:
            first_low, sides, other_addends = hold(first_low, sides, other_addends)
            pieces = scatter_pieces(line, sides)
            mlp_done[l + 1] = scatter_end(other_addends)
            first_low, pieces = hold(first_low, pieces)
            addends = scatter_far(pieces)
        (grad_mix,) = times_weight(
            relative_t, first_low, out, head_cols, lambda v: (v,), [], [BF], "grad_mix"
        )
        grad_mix, mlp_corners = hold(grad_mix, mlp_corners)
        mlp_sums = scatter_sum(mlp_line, mlp_corners)
        grad_mix, mlp_sums = hold(grad_mix, mlp_sums)
        mlp_sides = scatter_sides(mlp_sums)
        grad_proj = attend_back(projected, keys, head_cols, grad_mix, seg_q, seg_k)
        if sharers > 1:
            grad_proj = jnp.stack(
                [grad_proj[0]]
                + [
                    lax.psum_scatter(v, "tlo", scatter_dimension=0, tiled=True).astype(BF)
                    for v in grad_proj[1:]
                ]
            )
        left = dot(low, pick).astype(BF)
        attn_pairs = [(left, grad_proj), (turned(first_low), mixture[None])]
        attn_send = weight_grads(attn_pairs, blocks, 1, 2, name="attn_send")
        if flying is not None:
            attn_send, addends = hold(attn_send, addends)
            attn_done[l + 1] = scatter_end(addends)
        if l == 0:
            attn_send, grad_proj, mlp_sides = hold(attn_send, grad_proj, mlp_sides)
            mlp_pieces = scatter_pieces(mlp_line, mlp_sides)
            attn_send, grad_proj, mlp_pieces = hold(attn_send, grad_proj, mlp_pieces)
            mlp_addends = scatter_far(mlp_pieces)
        else:
            attn_send, grad_proj = hold(attn_send, grad_proj)
        attn_came = over_dp(attn_send, 1)
        if l > 0:
            back = times_transposed(relative_t, grad_proj, qkv, "grad_stream")
            back, attn_came = hold(back, attn_came)
        attn_line = weight_grads(
            attn_pairs, blocks, 0, 2, add=attn_came, blocks=2, name="attn_keep"
        )
        wide_grad = jnp.stack(
            [over_rows(grad_first), shift_early, over_rows(grad_second), shift_late]
        )
        gains_grad = jnp.stack([gain_early, gain_late])
        if l == 0:
            wide_grad, gains_grad = reorder(wide_grad, places), reorder(gains_grad, places)
        small_grads[l] = gains_grad, wide_grad, grad_proj, grad_pre
        if l == 0:
            attn_line, grad_proj = hold(attn_line, grad_proj)
            attn_corners = scatter_corners(attn_line)
            back = times_transposed(relative_t, grad_proj, qkv, "grad_stream")
            held = after(small_grads, back)
            heads_grads = [jnp.stack([over_rows(h[2][0]), over_rows(h[2][2])]) for h in held]
            ups_grads = jnp.stack([over_rows(h[3]) for h in held])
            attn_sums = scatter_sum(*after((attn_line, attn_corners), back))
            attn_sums, heads_grads, ups_grads = hold(attn_sums, heads_grads, ups_grads)
            attn_sides = scatter_sides(attn_sums)
            smalls = (
                jnp.stack([h[0] for h in held]),
                jnp.concatenate(
                    [
                        reorder(jnp.stack(heads_grads), relative_t),
                        jnp.stack([h[1] for h in held]),
                    ],
                    axis=1,
                ),
                reorder(ups_grads, relative_t),
            )
            small_sums = relative_small(
                jnp.concatenate([fold(whole) for whole in smalls], axis=1)
            )
            mlp_addends, small_sums = hold(mlp_addends, small_sums)
            mlp_done[l] = scatter_end(mlp_addends)
            small_sums = scatter_small(small_sums, 4 * blocks)
            attn_sides, small_sums = hold(attn_sides, small_sums)
            attn_pieces = scatter_pieces(attn_line, attn_sides)
            attn_pieces, small_sums = hold(attn_pieces, small_sums)
            attn_addends = scatter_far(attn_pieces)
            summed = scatter_small(small_sums, 1)[0]
            attn_done[l] = scatter_end(after(attn_addends, summed))
            input_grad = select_wide(after(grad_first, attn_sums), unpick) + back
        else:
            attn_line, back = hold(attn_line, back)
            flying = attn_line, scatter_corners(attn_line), mlp_line, mlp_sides
            grad_stream = grad_first + back

    return (
        stream.astype(BF),
        input_grad,
        jnp.stack(
            [
                jnp.stack(
                    [attn_done[l][:, k * head_cols : (k + 1) * head_cols] for k in range(3)]
                )
                for l in range(layers)
            ]
        ),
        jnp.stack([attn_done[l][:, 3 * head_cols :].T for l in range(layers)]),
        jnp.stack([mlp_done[l][:, :hidden] for l in range(layers)]),
        jnp.stack([mlp_done[l][:, hidden:].T for l in range(layers)]),
        summed[: cuts[0]].reshape(norm_gains.shape),
        summed[cuts[0] : cuts[1]].reshape(row_biases.shape),
        summed[cuts[1] :].reshape(ff_bias.shape),
    )


def solution(mesh):
    def whole(*args):
        inputs, seg_ids = args[:2]
        depth, blocks = mesh.shape["dp"], mesh.shape["tensor"]
        rows = inputs.shape[0] // (depth * blocks)
        sharers = max(1, seg_ids.shape[1] // rows)
        inner = Mesh(mesh.devices.reshape(depth, blocks // sharers, sharers), RANKS)
        tensor = ("thi", "tlo")
        row_wise = P(RANKS, None)
        weight_specs = (
            P(None, None, "dp", tensor),
            P(None, tensor, "dp"),
            P(None, "dp", tensor),
            P(None, tensor, "dp"),
            P(None, None, RANKS),
            P(None, None, RANKS),
            P(None, RANKS),
        )
        return jax.shard_map(
            on_device,
            mesh=inner,
            in_specs=(row_wise, P("dp", None)) + weight_specs + (row_wise,),
            out_specs=(row_wise, row_wise) + weight_specs,
            check_vma=False,
        )(*args)

    return whole
```

```python
from functools import partial

import jax
import jax.numpy as jnp
import numpy as np
from jax import lax
from jax.experimental import pallas as pl
from jax.experimental.pallas import tpu as pltpu
from jax.sharding import Mesh
from jax.sharding import PartitionSpec as P

HD = 64
EPSILON = 1e-06
HALF_ROOT = 0.7071067811865476
INV_ROOT_TAU = 0.3989422804014327
BF = jnp.bfloat16
F32 = jnp.float32
RANKS = ("dp", "thi", "tlo")
SPREAD = ("thi", "tlo", "dp")


def norm_parts(summed):
    centre = summed - jnp.mean(summed, axis=-1, keepdims=True)
    spread = jnp.mean(centre * centre, axis=-1, keepdims=True)
    rate = lax.rsqrt(spread + EPSILON)
    return centre * rate, rate


def norm_back(grad, unit, rate, gain):
    scaled = grad * gain
    return rate * (
        scaled
        - jnp.mean(scaled, axis=-1, keepdims=True)
        - unit * jnp.mean(scaled * unit, axis=-1, keepdims=True)
    )


def dot(a, b):
    return jnp.dot(a, b, preferred_element_type=F32)


def dot_nt(a, b):
    return lax.dot_general(a, b, (((1,), (1,)), ((), ())), preferred_element_type=F32)


def dot_tn(a, b):
    return lax.dot_general(a, b, (((0,), (0,)), ((), ())), preferred_element_type=F32)


def attend_kernel(q_ref, k_ref, v_ref, segq_ref, segk_ref, out_ref):
    same = segk_ref[0] == segq_ref[0]
    outs = []
    for half in range(q_ref.shape[1] // HD):
        cols = slice(half * HD, half * HD + HD)
        q = (q_ref[:, cols].astype(F32) * HD ** (-0.5)).astype(BF)
        scores = jnp.where(same, dot_nt(k_ref[:, cols], q), -jnp.inf)
        top = jnp.max(scores, axis=0, keepdims=True)
        weights = jnp.exp(scores - top)
        total = jnp.sum(weights, axis=0, keepdims=True)
        probs = (weights * (1.0 / total)).astype(BF)
        outs.append(dot_tn(probs, v_ref[:, cols]))
    out_ref[...] = jnp.concatenate(outs, axis=1).astype(BF)


def attend_back_kernel(q_ref, k_ref, v_ref, grad_ref, segq_ref, segk_ref, *out_refs):
    same = segk_ref[0] == segq_ref[0]
    found = [], [], []
    for half in range(q_ref.shape[1] // HD):
        cols = slice(half * HD, half * HD + HD)
        q = (q_ref[:, cols].astype(F32) * HD ** (-0.5)).astype(BF)
        k, v, grad = k_ref[:, cols], v_ref[:, cols], grad_ref[:, cols]
        scores = jnp.where(same, dot_nt(k, q), -jnp.inf)
        top = jnp.max(scores, axis=0, keepdims=True)
        weights = jnp.exp(scores - top)
        probs = weights * (1.0 / jnp.sum(weights, axis=0, keepdims=True))
        grad_probs = dot_nt(v, grad)
        inner = jnp.sum(grad_probs * probs, axis=0, keepdims=True)
        grad_scores = (probs * (grad_probs - inner)).astype(BF)
        found[0].append(dot_tn(grad_scores, k) * HD ** (-0.5))
        found[1].append(dot(grad_scores, q))
        found[2].append(dot(probs.astype(BF), grad))
    for i in range(3):
        target = out_refs[0].at[i] if len(out_refs) == 1 else out_refs[i]
        target[...] = jnp.concatenate(found[i], axis=1).astype(target.dtype)


def attention_specs(rows, keys, cols):
    wide = 128 if cols % 128 == 0 else cols
    pairs = cols // wide
    part = lambda n, k: pl.BlockSpec(
        (n, wide), lambda s, j: (s, (j // pairs * 3 + k) * pairs + j % pairs)
    )
    plain = lambda n: pl.BlockSpec((n, wide), lambda s, j: (s, j))
    segs = [
        pl.BlockSpec((1, 1, rows), lambda s, j: (s, 0, 0)),
        pl.BlockSpec((1, keys, 1), lambda s, j: (s, 0, 0)),
    ]
    return wide, pairs, [part(rows, 0), part(keys, 1), part(keys, 2)], plain, segs


def attend(q, kv, cols, seg_q, seg_k):
    sets, parts = seg_q.shape[0], q.shape[1] // (3 * cols)
    rows, keys = q.shape[0] // sets, kv.shape[0] // sets
    _, pairs, specs, plain, segs = attention_specs(rows, keys, cols)
    work = parts * cols // HD * sets * rows * keys
    return pl.pallas_call(
        attend_kernel,
        grid=(sets, parts * pairs),
        in_specs=specs + segs,
        out_specs=plain(rows),
        out_shape=jax.ShapeDtypeStruct((q.shape[0], parts * cols), BF),
        cost_estimate=pl.CostEstimate(
            flops=16 * work * HD, bytes_accessed=2 * q.size * 2, transcendentals=work
        ),
        name="attend",
    )(q, kv, kv, seg_q[:, None, :], seg_k[:, :, None])


def attend_back(q, kv, cols, grad, seg_q, seg_k):
    sets, parts = seg_q.shape[0], q.shape[1] // (3 * cols)
    rows, keys = q.shape[0] // sets, kv.shape[0] // sets
    wide, pairs, specs, plain, segs = attention_specs(rows, keys, cols)
    work = parts * cols // HD * sets * rows * keys
    if rows == keys:
        out_specs = pl.BlockSpec((3, rows, wide), lambda s, j: (0, s, j))
        out_shape = jax.ShapeDtypeStruct((3, q.shape[0], parts * cols), BF)
    else:
        out_specs = [plain(rows), plain(keys), plain(keys)]
        out_shape = [
            jax.ShapeDtypeStruct((q.shape[0], parts * cols), BF),
            jax.ShapeDtypeStruct((kv.shape[0], parts * cols), F32),
            jax.ShapeDtypeStruct((kv.shape[0], parts * cols), F32),
        ]
    return pl.pallas_call(
        attend_back_kernel,
        grid=(sets, parts * pairs),
        in_specs=specs + [plain(rows)] + segs,
        out_specs=out_specs,
        out_shape=out_shape,
        cost_estimate=pl.CostEstimate(
            flops=5 * work * HD, bytes_accessed=q.size, transcendentals=work // 8
        ),
        name="attend_back",
    )(q, kv, kv, grad, seg_q[:, None, :], seg_k[:, :, None])


def tile(most, *sizes):
    for size in (1024, 768, 512, 384, 256, 128):
        if size <= most and all(n % size == 0 for n in sizes):
            return size
    raise ValueError("width")


def cost(name, flops, *arrays):
    short = 1 if name in ("project", "attended", "enter", "branch") else 8
    return pl.CostEstimate(
        flops=flops // short,
        bytes_accessed=sum(a.size * a.dtype.itemsize for a in arrays) // short,
        transcendentals=0,
    )


def times_weight(which, x, weight, cols, finish, extras, out_types, name):
    rows, parts, count = x.shape[0], len(weight), len(weight[0])
    bn = tile(1024, cols, *[v[3] for w in weight for v in w])
    per = cols // bn

    def spec(t, view):
        _, block, height, first = view
        local = lambda j: first // bn + jnp.clip(j - t * per, 0, per - 1)
        if block is None:
            return pl.BlockSpec((height, bn), lambda j, _: (0, local(j)))
        return pl.BlockSpec((height, bn), lambda j, names: (names[block], local(j)))

    def kernel(which_ref, x_ref, *refs):
        step = pl.program_id(0)
        more = refs[parts * count : parts * count + len(extras)]
        outs = refs[parts * count + len(extras) :]
        for t in range(parts):

            @pl.when((step >= t * per) & (step < t * per + per))
            def _(t=t):
                total, first = None, 0
                for ref in refs[t * count : (t + 1) * count]:
                    height = ref.shape[0]
                    part = dot(x_ref[:, first : first + height], ref[...])
                    total = part if total is None else total + part
                    first += height
                for ref, out in zip(outs, finish(total, *[e[...] for e in more])):
                    ref[...] = out.astype(ref.dtype)

    return pl.pallas_call(
        kernel,
        grid_spec=pltpu.PrefetchScalarGridSpec(
            num_scalar_prefetch=1,
            grid=(parts * per,),
            in_specs=[pl.BlockSpec(x.shape, lambda j, _: (0, 0))]
            + [spec(t, v) for t in range(parts) for v in weight[t]]
            + [pl.BlockSpec((e.shape[0], bn), lambda j, _: (0, j)) for e in extras],
            out_specs=[pl.BlockSpec((rows, bn), lambda j, _: (0, j)) for _ in out_types],
        ),
        out_shape=[jax.ShapeDtypeStruct((rows, parts * cols), t) for t in out_types],
        cost_estimate=cost(name, 2 * x.size * cols * parts, x, x),
        name=name,
    )(which, x, *[v[0] for w in weight for v in w], *extras)


def times_transposed(which, right, weight, name):
    parts = len(weight)
    stack, rows, each = right.shape[0], right.shape[1], right.shape[2] // parts
    bn = tile(1024, each, *[v[3] for w in weight for v in w])
    per = each // bn
    heights = [v[2] for v in weight[0]]
    width = sum(heights)

    def spec(view):
        _, block, height, first = view
        if block is None:
            return pl.BlockSpec((height, bn), lambda j, _: (0, first // bn + j))
        return pl.BlockSpec((height, bn), lambda j, names: (names[block], first // bn + j))

    def kernel(which_ref, *refs):
        out_ref = refs[-1]

        @pl.when(pl.program_id(0) == 0)
        def _():
            out_ref[...] = jnp.zeros_like(out_ref)

        place = 0
        for b, height in enumerate(heights):
            cols = slice(place, place + height)
            total = out_ref[:, cols]
            for t in range(parts):
                total += dot_nt(refs[t][...], refs[parts + t * len(heights) + b][...])
            out_ref[:, cols] = total
            place += height

    return pl.pallas_call(
        kernel,
        grid_spec=pltpu.PrefetchScalarGridSpec(
            num_scalar_prefetch=1,
            grid=(stack * per,),
            in_specs=[
                pl.BlockSpec(
                    (None, rows, bn), lambda j, _, t=t: (j // per, 0, t * per + j % per)
                )
                for t in range(parts)
            ]
            + [spec(v) for w in weight for v in w],
            out_specs=pl.BlockSpec((rows, width), lambda j, _: (0, 0)),
        ),
        out_shape=jax.ShapeDtypeStruct((rows, width), F32),
        cost_estimate=cost(name, 2 * rows * width * stack * each * parts, right),
        name=name,
    )(which, *[right] * parts, *[v[0] for w in weight for v in w])


def weight_grads(pairs, parts, section, sections, add=None, blocks=1, name="weight_grads"):
    rows, width = pairs[0][0].shape
    height = width // sections
    bn = tile(1024, *[right.shape[2] // parts for _, right in pairs])
    counts = [right.shape[0] * right.shape[2] // parts // bn for _, right in pairs]
    starts = [sum(counts[:i]) for i in range(len(pairs))]
    columns = sum(counts) * bn
    low = height // blocks

    def kernel(*refs):
        step = pl.program_id(0)
        turned = refs[-len(pairs) :]
        at = len(pairs) * (1 + parts)
        add_ref = refs[at] if add is not None else None
        outs = refs[at + (add is not None) : -len(pairs)]
        for i in range(len(pairs)):
            base = i * (1 + parts)

            @pl.when(step == starts[i])
            def _(i=i, base=base):
                turned[i][...] = refs[base][...].T

            @pl.when((step >= starts[i]) & (step < starts[i] + counts[i]))
            def _(i=i, base=base):
                for t in range(parts):
                    value = dot(turned[i][...], refs[base + 1 + t][...])
                    if add_ref is not None:
                        value += add_ref[t].astype(F32)
                    value = value.astype(BF)
                    if blocks == 1:
                        outs[0][t] = value
                    else:
                        for b in range(blocks):
                            outs[b * parts + t][...] = value[b * low : (b + 1) * low]

    in_specs, operands = [], []
    for i, (left, right) in enumerate(pairs):
        in_specs.append(pl.BlockSpec((rows, height), lambda j: (0, section)))
        operands.append(left)
        per = right.shape[2] // parts // bn
        for t in range(parts):

            def where(j, i=i, t=t, per=per):
                local = jnp.clip(j - starts[i], 0, counts[i] - 1)
                return local // per, 0, t * per + local % per

            in_specs.append(pl.BlockSpec((None, rows, bn), where))
            operands.append(right)
    if add is not None:
        in_specs.append(pl.BlockSpec((parts, height, bn), lambda j: (0, 0, j)))
        operands.append(add)
    if blocks == 1:
        out_specs = pl.BlockSpec((parts, height, bn), lambda j: (0, 0, j))
        out_shape = jax.ShapeDtypeStruct((parts, height, columns), BF)
    else:
        out_specs = [pl.BlockSpec((low, bn), lambda j: (0, j))] * (blocks * parts)
        out_shape = [jax.ShapeDtypeStruct((low, columns), BF)] * (blocks * parts)
    found = pl.pallas_call(
        kernel,
        grid=(sum(counts),),
        in_specs=in_specs,
        out_specs=out_specs,
        out_shape=out_shape,
        scratch_shapes=[pltpu.VMEM((height, rows), BF) for _ in pairs],
        cost_estimate=cost(name, 2 * height * rows * columns * parts, *[p[1] for p in pairs]),
        name=name,
    )(*operands)
    if blocks == 1:
        return found
    return [[found[b * parts + t] for t in range(parts)] for b in range(blocks)]


def three_parts(value):
    first = lax.reduce_precision(value, 8, 7)
    second = lax.reduce_precision(value - first, 8, 7)
    return [part.astype(BF) for part in (first, second, value - first - second)]


def pack_small(row, height):
    flat = jnp.concatenate(three_parts(row))
    columns = -(-flat.shape[0] // (128 * height)) * 128
    return jnp.pad(flat, (0, height * columns - flat.shape[0])).reshape(height, columns)


def unpack_small(packed, size, height):
    depth = lax.axis_size("dp")
    flat = packed.reshape(-1, depth, height * packed.shape[1])[:, :, : 3 * size]
    parts = jnp.sum(flat.reshape(-1, depth, 3, size).astype(F32), axis=2)
    return jnp.swapaxes(parts, 0, 1).reshape(-1, size)


def swap(value, mask):
    count = lax.axis_size("dp") * lax.axis_size("thi") * lax.axis_size("tlo")
    return lax.ppermute(value, RANKS, [(i, i ^ mask) for i in range(count)])


def relative_small(parts):
    return jnp.take(parts, jnp.arange(parts.shape[0]) ^ lax.axis_index(RANKS), axis=0)


def scatter_small(held, until):
    mask = held.shape[0] // 2
    while mask >= until:
        held = held[:mask] + swap(held[mask:], mask)
        mask //= 2
    return held


def over_dp(value, mask):
    count = lax.axis_size("dp")
    return lax.ppermute(value, "dp", [(i, i ^ mask) for i in range(count)])


def over_tensor(value, mask):
    count = lax.axis_size("thi") * lax.axis_size("tlo")
    return lax.ppermute(value, ("thi", "tlo"), [(i, i ^ mask) for i in range(count)])


def tensor_size():
    return lax.axis_size("thi") * lax.axis_size("tlo")


def hold(*trees):
    return lax.optimization_barrier(trees)


def after(tree, *others):
    return lax.optimization_barrier((tree, others))[0]


def gather_far(shard):
    rest = lax.axis_size("dp") // 4
    return jnp.concatenate([shard] + [over_dp(shard, 4 * m) for m in range(1, rest)], axis=0)


def gather_sides(own):
    return over_dp(own, 2), [over_tensor(own, m) for m in range(1, tensor_size())]


def gather_corners(own, sides):
    across, near = sides
    half = own.shape[0] // 2
    far = [
        jnp.concatenate([over_dp(block[:half], 2), over_tensor(across[half:], m + 1)], axis=0)
        for m, block in enumerate(near)
    ]
    return [[own] + near, [across] + far]


def gather_core(here):
    return [here, [[over_dp(block, 1) for block in line] for line in here]]


def block_views(blocks, first):
    return [
        [(line[t], None, line[t].shape[0], first) for half in blocks for line in half]
        for t in range(len(blocks[0][0]))
    ]


def wide(value):
    return value.astype(F32)


def scatter_corners(line):
    half = line[0][0].shape[0] // 2
    return (
        [over_dp(block[:half], 2) for block in line[1][1:]],
        [over_tensor(block[half:], m + 1) for m, block in enumerate(line[1][1:])],
    )


def scatter_sum(line, corners):
    near, across = line[0][1:], line[1][0]
    half = across.shape[0] // 2
    tops, bottoms = corners
    near = [
        jnp.concatenate([(wide(a[:half]) + wide(b)).astype(BF), a[half:]], axis=0)
        for a, b in zip(near, tops)
    ]
    if bottoms:
        low = (wide(across[half:]) + sum(wide(b) for b in bottoms)).astype(BF)
        across = jnp.concatenate([across[:half], low], axis=0)
    return [across] + near


def scatter_sides(sums):
    return [over_dp(sums[0], 2)] + [over_tensor(v, m + 1) for m, v in enumerate(sums[1:])]


def scatter_pieces(line, sides):
    own = line[0][0]
    rest = lax.axis_size("dp") // 4
    height = own.shape[0] // rest
    piece = lambda m: sum(
        (wide(v[m * height : (m + 1) * height]) for v in sides),
        wide(own[m * height : (m + 1) * height]),
    )
    return [piece(0)] + [piece(m).astype(BF) for m in range(1, rest)]


def scatter_far(pieces):
    return [pieces[0]] + [over_dp(piece, 4 * m) for m, piece in enumerate(pieces) if m]


def scatter_end(addends):
    return sum(wide(v) for v in addends)


def relative_blocks():
    depth = lax.axis_size("dp")
    rest = depth // 4
    own = lax.axis_index("dp")
    place = np.arange(depth)
    core, second, far = place // (2 * rest), place // rest % 2, place % rest
    order = jnp.asarray(far * 4 + second * 2 + core) ^ own
    mask = jnp.arange(depth) ^ own
    places = ((mask & 1) * 2 + (mask >> 1 & 1)) * rest + (mask >> 2)
    return order, places


def reorder(rows, order):
    cut = rows.reshape(rows.shape[:-1] + (order.shape[0], -1))
    return jnp.take(cut, order, axis=-2).reshape(rows.shape)


def selection(order, width):
    each = width // order.shape[0]
    source = (order[:, None] * each + jnp.arange(each)[None]).reshape(-1)
    return (jnp.arange(width)[:, None] == source[None, :]).astype(BF)


def select_wide(rows, chooser):
    return sum(dot(part, chooser) for part in three_parts(rows))


def on_device(
    inputs,
    seg_ids,
    qkv_weight,
    out_weight,
    up_weight,
    down_weight,
    norm_gains,
    row_biases,
    ff_bias,
    cotangent,
):
    blocks = tensor_size()
    sharers = lax.axis_size("tlo")
    rows, width = inputs.shape
    layers = qkv_weight.shape[0]
    head_cols = qkv_weight.shape[3]
    hidden = up_weight.shape[2]
    length = seg_ids.shape[1]
    sets = max(1, rows // length)
    T = range(blocks)

    seg_k = lax.dynamic_slice_in_dim(seg_ids, lax.axis_index("thi") * sets, sets)
    seg_q = seg_k
    if sharers > 1:
        seg_q = lax.dynamic_slice_in_dim(seg_k, lax.axis_index("tlo") * rows, rows, axis=1)

    order, places = relative_blocks()
    pick, unpick = selection(order, width), selection(places, width)
    own_t = lax.axis_index(("thi", "tlo"))
    relative_t = (jnp.arange(blocks, dtype=jnp.int32) ^ own_t).astype(jnp.int32)

    join = lambda *parts: jnp.concatenate(parts, axis=1).astype(BF)
    qkv_of = lambda l: [qkv_weight[l, k] for k in range(3)]
    spread = lambda shard: lax.all_gather(shard, SPREAD, axis=0, tiled=True)
    views = lambda whole, first: [[(whole, t, width, first)] for t in T]
    row = jnp.concatenate([norm_gains.reshape(-1), row_biases.reshape(-1), ff_bias.reshape(-1)])
    height = qkv_weight.shape[2]
    first_whole = spread(jnp.concatenate([join(*qkv_of(0)), pack_small(row, height)], axis=1))
    small = unpack_small(first_whole[:, 3 * head_cols :], row.shape[0], height)
    later_views = [None]
    for l in range(1, layers):
        whole = spread(join(*qkv_of(l), out_weight[l].T, up_weight[l], down_weight[l].T))
        firsts = (0, 3 * head_cols, 4 * head_cols, 4 * head_cols + hidden)
        later_views.append([views(whole, first) for first in firsts])
    mid_own = gather_far(join(up_weight[0], out_weight[0].T))
    down_shard = join(down_weight[0].T)
    mid_own, down_shard = hold(mid_own, down_shard)
    mid_sides = gather_sides(mid_own)
    down_own = gather_far(down_shard)
    mid_here = gather_corners(mid_own, mid_sides)
    mid_blocks = gather_core(mid_here)
    down_own, mid_here = hold(down_own, mid_here)
    down_sides = gather_sides(down_own)

    devices = small.shape[0]
    cuts = np.cumsum([norm_gains.size, row_biases.size])
    spread_out = lambda piece, like: jnp.moveaxis(
        piece.reshape((devices,) + like.shape), 0, -2
    ).reshape(like.shape[:-1] + (devices * like.shape[-1],))
    gain_rows = spread_out(small[:, : cuts[0]], norm_gains)
    shift_rows = spread_out(small[:, cuts[0] : cuts[1]], row_biases)
    up_shifts = spread_out(small[:, cuts[1] :], ff_bias)

    def vectors(l):
        gains, shifts, up_shift = gain_rows[l], shift_rows[l], up_shifts[l]
        heads, wide = reorder(shifts[:2], relative_t), shifts[2:]
        up_shift = reorder(up_shift, relative_t)
        if l == 0:
            gains, wide = reorder(gains, order), reorder(wide, order)
        heads = heads.reshape(2, blocks, head_cols)
        qkv_shift = jnp.stack([heads[0], jnp.zeros_like(heads[0]), heads[1]], axis=1)
        return gains, qkv_shift.reshape(1, -1), wide, up_shift[None]

    add_shift = lambda value, shift: (value + shift,)

    def enter(value, shift):
        value = value + shift
        upto = 0.5 * (1.0 + lax.erf(value * HALF_ROOT))
        return value * upto, upto + value * jnp.exp(-0.5 * value * value) * INV_ROOT_TAU

    def leave(value, slope):
        return (value * slope.astype(F32),)

    gather_keys = (
        (lambda v: lax.all_gather(v, "tlo", axis=0, tiled=True)) if sharers > 1 else (lambda v: v)
    )
    stored = []
    stream = dot(inputs, pick)
    for l in range(layers):
        gains, qkv_shift, shifts, up_shift = vectors(l)
        if l == 1:
            stream = select_wide(stream, unpick)
        if l == 0:
            qkv, low = views(first_whole, 0), inputs
        else:
            qkv, out, up, down = later_views[l]
            low = stream.astype(BF)
        (projected,) = times_weight(
            relative_t, low, qkv, 3 * head_cols, add_shift, [qkv_shift], [BF], "project"
        )
        if l == 0:
            projected, down_sides = hold(projected, down_sides)
            down_here = gather_corners(down_own, down_sides)
        keys = gather_keys(projected)
        mixture = attend(projected, keys, head_cols, seg_q, seg_k)
        if l == 0:
            mixture, down_here = hold(mixture, down_here)
            up, out = block_views(mid_blocks, 0), block_views(mid_blocks, hidden)
            down = block_views(gather_core(down_here), 0)
        attended = times_transposed(relative_t, mixture[None], out, "attended")
        unit_early, rate_early = norm_parts(stream + (attended + shifts[0]))
        mid = unit_early * gains[0] + shifts[1]
        mid_low = mid.astype(BF)
        hidden_out, slopes = times_weight(
            relative_t, mid_low, up, hidden, enter, [up_shift], [BF, BF], "enter"
        )
        branch = times_transposed(relative_t, hidden_out[None], down, "branch")
        unit_late, rate_late = norm_parts(mid + (branch + shifts[2]))
        stored.append(
            (
                qkv,
                out,
                up,
                down,
                gains,
                low,
                projected,
                keys,
                mixture,
                unit_early,
                rate_early,
                mid_low,
                slopes,
                hidden_out,
                unit_late,
                rate_late,
            )
        )
        stream = unit_late * gains[1] + shifts[3]
    if layers == 1:
        stream = select_wide(stream, unpick)

    grad_stream = cotangent
    mlp_done, attn_done = [None] * layers, [None] * layers
    small_grads = [None] * layers
    over_rows = lambda value: jnp.sum(value.astype(F32), axis=0)
    fold = lambda whole: jnp.moveaxis(
        whole.reshape(whole.shape[:-1] + (devices, whole.shape[-1] // devices)), -2, 0
    ).reshape(devices, -1)
    flying = None
    for l in reversed(range(layers)):
        (
            qkv,
            out,
            up,
            down,
            gains,
            low,
            projected,
            keys,
            mixture,
            unit_early,
            rate_early,
            mid_low,
            slopes,
            hidden_out,
            unit_late,
            rate_late,
        ) = stored[l]
        if l == 0:
            grad_stream = select_wide(grad_stream, pick)
        grad_second = norm_back(grad_stream, unit_late, rate_late, gains[1])
        gain_late, shift_late = over_rows(grad_stream * unit_late), over_rows(grad_stream)
        second_low = grad_second.astype(BF)
        (grad_pre,) = times_weight(relative_t, second_low, down, hidden, leave, [slopes], [BF], "leave")
        if flying is not None:
            line, corners, other_addends = flying
            grad_pre, corners = hold(grad_pre, corners)
            sums = scatter_sum(line, corners)
            grad_pre, sums = hold(grad_pre, sums)
            sides = scatter_sides(sums)
        turned = (lambda v: v) if l == 0 else (lambda v: dot(v, pick).astype(BF))
        mlp_pairs = [(turned(mid_low), grad_pre[None]), (turned(second_low), hidden_out[None])]
        mlp_send = weight_grads(mlp_pairs, blocks, 1, 2, name="mlp_send")
        mlp_send, grad_pre = hold(mlp_send, grad_pre)
        mlp_came = over_dp(mlp_send, 1)
        back = times_transposed(relative_t, grad_pre[None], up, "grad_mid")
        mlp_line = weight_grads(
            mlp_pairs, blocks, 0, 2, add=after(mlp_came, back), blocks=2, name="mlp_keep"
        )
        mlp_line, back = hold(mlp_line, back)
        mlp_corners = scatter_corners(mlp_line)
        grad_mid = grad_second + back
        grad_first = norm_back(grad_mid, unit_early, rate_early, gains[0])
        gain_early, shift_early = over_rows(grad_mid * unit_early), over_rows(grad_mid)
        first_low = grad_first.astype(BF)
        if flying is not None:
            first_low, sides, other_addends = hold(first_low, sides, other_addends)
            pieces = scatter_pieces(line, sides)
            mlp_done[l + 1] = scatter_end(other_addends)
            first_low, pieces = hold(first_low, pieces)
            addends = scatter_far(pieces)
        (grad_mix,) = times_weight(
            relative_t, first_low, out, head_cols, lambda v: (v,), [], [BF], "grad_mix"
        )
        grad_mix, mlp_corners = hold(grad_mix, mlp_corners)
        mlp_sums = scatter_sum(mlp_line, mlp_corners)
        grad_mix, mlp_sums = hold(grad_mix, mlp_sums)
        mlp_sides = scatter_sides(mlp_sums)
        grad_proj = attend_back(projected, keys, head_cols, grad_mix, seg_q, seg_k)
        if sharers > 1:
            grad_proj = jnp.stack(
                [grad_proj[0]]
                + [
                    lax.psum_scatter(v, "tlo", scatter_dimension=0, tiled=True).astype(BF)
                    for v in grad_proj[1:]
                ]
            )
        left = dot(low, pick).astype(BF)
        attn_pairs = [(left, grad_proj), (turned(first_low), mixture[None])]
        attn_send = weight_grads(attn_pairs, blocks, 1, 2, name="attn_send")
        if flying is not None:
            attn_send, addends = hold(attn_send, addends)
            attn_done[l + 1] = scatter_end(addends)
        attn_send, grad_proj, mlp_sides = hold(attn_send, grad_proj, mlp_sides)
        mlp_pieces = scatter_pieces(mlp_line, mlp_sides)
        attn_send, grad_proj, mlp_pieces = hold(attn_send, grad_proj, mlp_pieces)
        mlp_addends = scatter_far(mlp_pieces)
        attn_came = over_dp(attn_send, 1)
        if l > 0:
            back = times_transposed(relative_t, grad_proj, qkv, "grad_stream")
            back, attn_came = hold(back, attn_came)
        attn_line = weight_grads(
            attn_pairs, blocks, 0, 2, add=attn_came, blocks=2, name="attn_keep"
        )
        wide_grad = jnp.stack(
            [over_rows(grad_first), shift_early, over_rows(grad_second), shift_late]
        )
        gains_grad = jnp.stack([gain_early, gain_late])
        if l == 0:
            wide_grad, gains_grad = reorder(wide_grad, places), reorder(gains_grad, places)
        small_grads[l] = gains_grad, wide_grad, grad_proj, grad_pre
        if l == 0:
            attn_line, grad_proj = hold(attn_line, grad_proj)
            attn_corners = scatter_corners(attn_line)
            back = times_transposed(relative_t, grad_proj, qkv, "grad_stream")
            held = after(small_grads, back)
            heads_grads = [jnp.stack([over_rows(h[2][0]), over_rows(h[2][2])]) for h in held]
            ups_grads = jnp.stack([over_rows(h[3]) for h in held])
            attn_sums = scatter_sum(*after((attn_line, attn_corners), back))
            attn_sums, heads_grads, ups_grads = hold(attn_sums, heads_grads, ups_grads)
            attn_sides = scatter_sides(attn_sums)
            smalls = (
                jnp.stack([h[0] for h in held]),
                jnp.concatenate(
                    [
                        reorder(jnp.stack(heads_grads), relative_t),
                        jnp.stack([h[1] for h in held]),
                    ],
                    axis=1,
                ),
                reorder(ups_grads, relative_t),
            )
            small_sums = relative_small(
                jnp.concatenate([fold(whole) for whole in smalls], axis=1)
            )
            mlp_addends, small_sums = hold(mlp_addends, small_sums)
            mlp_done[l] = scatter_end(mlp_addends)
            small_sums = scatter_small(small_sums, 4 * blocks)
            attn_sides, small_sums = hold(attn_sides, small_sums)
            attn_pieces = scatter_pieces(attn_line, attn_sides)
            attn_pieces, small_sums = hold(attn_pieces, small_sums)
            attn_addends = scatter_far(attn_pieces)
            summed = scatter_small(small_sums, 1)[0]
            attn_done[l] = scatter_end(after(attn_addends, summed))
            input_grad = select_wide(after(grad_first, attn_sums), unpick) + back
        else:
            attn_line, back = hold(attn_line, back)
            flying = attn_line, scatter_corners(attn_line), mlp_addends
            grad_stream = grad_first + back

    return (
        stream.astype(BF),
        input_grad,
        jnp.stack(
            [
                jnp.stack(
                    [attn_done[l][:, k * head_cols : (k + 1) * head_cols] for k in range(3)]
                )
                for l in range(layers)
            ]
        ),
        jnp.stack([attn_done[l][:, 3 * head_cols :].T for l in range(layers)]),
        jnp.stack([mlp_done[l][:, :hidden] for l in range(layers)]),
        jnp.stack([mlp_done[l][:, hidden:].T for l in range(layers)]),
        summed[: cuts[0]].reshape(norm_gains.shape),
        summed[cuts[0] : cuts[1]].reshape(row_biases.shape),
        summed[cuts[1] :].reshape(ff_bias.shape),
    )


def solution(mesh):
    def whole(*args):
        inputs, seg_ids = args[:2]
        depth, blocks = mesh.shape["dp"], mesh.shape["tensor"]
        rows = inputs.shape[0] // (depth * blocks)
        sharers = max(1, seg_ids.shape[1] // rows)
        inner = Mesh(mesh.devices.reshape(depth, blocks // sharers, sharers), RANKS)
        tensor = ("thi", "tlo")
        row_wise = P(RANKS, None)
        weight_specs = (
            P(None, None, "dp", tensor),
            P(None, tensor, "dp"),
            P(None, "dp", tensor),
            P(None, tensor, "dp"),
            P(None, None, RANKS),
            P(None, None, RANKS),
            P(None, RANKS),
        )
        return jax.shard_map(
            on_device,
            mesh=inner,
            in_specs=(row_wise, P("dp", None)) + weight_specs + (row_wise,),
            out_specs=(row_wise, row_wise) + weight_specs,
            check_vma=False,
        )(*args)

    return whole
```
